32 devices in a mesh: brick: 8 (over y, x, core), help: 4 (over z).
Axes of the slice: x: 2, y: 2, z: 4, core: 2. Of those that a mesh axis runs over, the one named last changes fastest.
Arguments:
- positions: float32 [3, 2048], P(None, ('brick', 'help')), may hold values from 0 to 1
- velocities: float32 [3, 2048], P(None, ('brick', 'help')), may hold values from -5 to 5
- forces_in: float32 [3, 2048], P(None, ('brick', 'help')), may hold values from -5 to 5
- neighbors: int32 [2048, 128], P(('brick', 'help')), may hold values from -1 to 767, as said below
- w_embed1: float32 [32], replicated, may hold values from -4 to 4
- b_embed1: float32 [32], replicated, may hold values from -3 to 3
- w_embed2: bfloat16 [32, 64], replicated, may hold values from -1 to 1
- b_embed2: float32 [64], replicated, may hold values from -3 to 3
- w_embed3: bfloat16 [64, 128], replicated, may hold values from -0.75 to 0.75
- b_embed3: float32 [128], replicated, may hold values from -3 to 3
- w_fit1: bfloat16 [2048, 240], replicated, may hold values from -0.125 to 0.125
- b_fit1: float32 [240], replicated, may hold values from -3 to 3
- w_fit2: bfloat16 [240, 240], replicated, may hold values from -0.375 to 0.375
- b_fit2: float32 [240], replicated, may hold values from -3 to 3
- w_out: float32 [240], replicated, may hold values from -0.375 to 0.375
Outputs:
- positions_out: float32 [3, 2048], P(None, ('brick', 'help'))
- velocities_out: float32 [3, 2048], P(None, ('brick', 'help'))
- energy: float32 [2048], P(('brick', 'help'))
- forces_out: float32 [3, 2048], P(None, ('brick', 'help'))
The draws below stay inside these ranges and needn't reach their ends.
Inputs may be any that keep to these rules, and one draw needn't show every extreme that they name: `neighbors`: row i holds atom i's neighbours as table entries: 0 to 255 the atoms of the brick before its own (cyclically), 256 to 511 its own brick, 512 to 767 the brick after; -1 pads. Live entries come first, an entry may repeat, an atom never lists itself. In the first half of the bricks an atom has 96 to 128 live entries, in the other bricks 128 / 4 to 64.
All inputs are finite; a program needn't handle non-finite values.
Results may differ from the reference program's by a relative error of at most 0.011.
Values sent between devices are 32-bit elements; how exact they have to be, the bound alone decides.
No kernel may reach another device: no remote copies, remote signals or barrier semaphores. Data moves between devices by JAX's collectives and lax.ppermute only.
A program may use at most 64 MiB of HBM per device.

```python
import jax
import jax.numpy as jnp
from jax import lax

ATOM_DEV = 64
NEIGHBOUR_SLOTS = 128
E1 = 32
E2 = 64
E3 = 128
M2 = 16
FIT = 240
STEPS = 2
BRICK = 256
ATOMS = 2048
N_BRICK = 8


def draw_neighbors(key, part):
    keys = jax.random.split(jax.random.fold_in(key, 7), 4)
    row_ids = jnp.arange(ATOMS, dtype=jnp.int32)
    dense = row_ids // BRICK < (ATOMS // BRICK + 1) // 2
    lower = jnp.where(dense, 3 * NEIGHBOUR_SLOTS // 4, NEIGHBOUR_SLOTS // 4).astype(jnp.int32)
    upper = (jnp.where(dense, NEIGHBOUR_SLOTS, NEIGHBOUR_SLOTS // 2) + 1).astype(jnp.int32)
    live_count = jax.random.randint(keys[0], (ATOMS,), lower, upper, dtype=jnp.int32)
    region = jax.random.randint(keys[1], (ATOMS, NEIGHBOUR_SLOTS), 0, 4, dtype=jnp.int32)
    own_pick = jax.random.randint(keys[2], (ATOMS, NEIGHBOUR_SLOTS), 0, BRICK - 1, dtype=jnp.int32)
    ghost_pick = jax.random.randint(keys[3], (ATOMS, NEIGHBOUR_SLOTS), 0, BRICK, dtype=jnp.int32)
    local = (row_ids % BRICK)[:, None]
    own_pick = jnp.where(own_pick >= local, own_pick + 1, own_pick)
    table_index = jnp.where(region == 0, ghost_pick, jnp.where(region == 1, 2 * BRICK + ghost_pick, BRICK + own_pick))
    slot_ids = jnp.arange(NEIGHBOUR_SLOTS, dtype=jnp.int32)[None, :]
    table_index = jnp.where(slot_ids < live_count[:, None], table_index, -1)
    table_index = table_index.at[0, 0].set(3 * BRICK - 1)
    return table_index.astype(jnp.int32)


def block_scale(key, shape, shards, least, high):
    loudness = 1.0
    for axis_at, parts in shards:
        draws = jax.random.uniform(jax.random.fold_in(jax.random.fold_in(key, 6), axis_at), (parts,), jnp.float32, least / len(shards), high / len(shards))
        loudness = loudness * jnp.repeat(jnp.exp(draws), shape[axis_at] // parts).reshape((-1,) + (1,) * (len(shape) - 1 - axis_at))
    return loudness


def noise(key, dims, spread, most, cuts=(), kind=jnp.bfloat16):
    drawn = jax.random.normal(key, dims, jnp.float32) * spread
    if len(cuts) > 0:
        drawn = block_scale(key, dims, cuts, -0.22, 0.18) * drawn
    return jnp.clip(drawn, min=-most, max=most).astype(kind)


def setup_inputs(seed: int = 0) -> dict:
    splits = jax.random.split(jax.random.key(seed), 16)
    positions = jnp.clip(1.0 * jax.random.uniform(splits[0], (3, ATOMS), jnp.float32) ** block_scale(splits[0], (3, ATOMS), ((1, 32),), -0.2, 0.2), 0.0, 1.0)
    velocities = noise(splits[1], (3, ATOMS), 1.0, 5.0, ((1, 32),), jnp.float32)
    forces_in = noise(splits[2], (3, ATOMS), 1.0, 5.0, ((1, 32),), jnp.float32)
    neighbors = draw_neighbors(jax.random.fold_in(splits[15], 71), 0)
    w_embed1 = noise(splits[4], (E1,), 1.0, 4.0, (), jnp.float32)
    b_embed1 = noise(splits[5], (E1,), 0.5, 3.0, (), jnp.float32)
    w_embed2 = noise(splits[6], (E1, E2), E1 ** -0.5, 1.0)
    b_embed2 = noise(splits[7], (E2,), 0.5, 3.0, (), jnp.float32)
    w_embed3 = noise(splits[8], (E2, E3), E2 ** -0.5, 0.75)
    b_embed3 = noise(splits[9], (E3,), 0.5, 3.0, (), jnp.float32)
    w_fit1 = noise(splits[10], (E3 * M2, FIT), (E3 * M2) ** -0.5, 0.125)
    b_fit1 = noise(splits[11], (FIT,), 0.5, 3.0, (), jnp.float32)
    w_fit2 = noise(splits[12], (FIT, FIT), FIT ** -0.5, 0.375)
    b_fit2 = noise(splits[13], (FIT,), 0.5, 3.0, (), jnp.float32)
    w_out = noise(splits[14], (FIT,), FIT ** -0.5, 0.375, (), jnp.float32)
    return {"positions": positions, "velocities": velocities, "forces_in": forces_in, "neighbors": neighbors, "w_embed1": w_embed1, "b_embed1": b_embed1, "w_embed2": w_embed2, "b_embed2": b_embed2, "w_embed3": w_embed3, "b_embed3": b_embed3, "w_fit1": w_fit1, "b_fit1": b_fit1, "w_fit2": w_fit2, "b_fit2": b_fit2, "w_out": w_out}


kick_scale = 0.25
time_step = 0.05
highest_precision = lax.Precision.HIGHEST

def pair_terms(displace, live_mask, weights):
    w_embed1, b_embed1, w_embed2, b_embed2, w_embed3, b_embed3, w_fit1, b_fit1, w_fit2, b_fit2, w_out = weights
    blocks, slot_count = live_mask.shape
    quad_dist = lax.optimization_barrier(jnp.sum(displace * displace, axis=0)) + 0.25
    radius = jnp.sqrt(quad_dist)
    smooth = live_mask / radius
    environment_matrix = jnp.concatenate([smooth[None], live_mask[None] * displace / quad_dist[None]], axis=0).astype(jnp.bfloat16)
    flat_smooth = smooth.reshape(1, -1)
    hidden_first = jnp.tanh(w_embed1[:, None] * flat_smooth + b_embed1[:, None])
    pre_second = jnp.dot(w_embed2.T, hidden_first.astype(jnp.bfloat16), preferred_element_type=jnp.float32) + b_embed2[:, None]
    tanh_second = jnp.tanh(pre_second)
    hidden_second = jnp.concatenate([hidden_first, hidden_first], axis=0) + tanh_second
    pre_third = jnp.dot(w_embed3.T, hidden_second.astype(jnp.bfloat16), preferred_element_type=jnp.float32) + b_embed3[:, None]
    tanh_third = jnp.tanh(pre_third)
    embedding = (jnp.concatenate([hidden_second, hidden_second], axis=0) + tanh_third).astype(jnp.bfloat16)
    embedding_width = embedding.shape[0]
    embedding_rows = embedding.reshape(embedding_width, blocks, slot_count)
    descriptor_tensor = jnp.einsum('srj,lrj->rsl', environment_matrix.astype(jnp.float32), embedding_rows.astype(jnp.float32), precision=highest_precision) / NEIGHBOUR_SLOTS
    axis_part = descriptor_tensor[:, :, :M2]
    descriptor = jnp.einsum('bce,bck->bek', descriptor_tensor, axis_part, precision=highest_precision)
    flat_descr = descriptor.reshape(blocks, -1).astype(jnp.bfloat16)
    fit_hidden = jnp.tanh(jnp.dot(flat_descr, w_fit1, preferred_element_type=jnp.float32) + b_fit1)
    pre_out = jnp.dot(fit_hidden.astype(jnp.bfloat16), w_fit2, preferred_element_type=jnp.float32) + b_fit2
    tanh_out = jnp.tanh(pre_out)
    energy = jnp.dot(fit_hidden + tanh_out, w_out, precision=highest_precision)
    grad_out = (w_out[None, :] * (1.0 - tanh_out * tanh_out)).astype(jnp.bfloat16)
    grad_fit = w_out[None, :] + jnp.dot(grad_out, w_fit2.T, preferred_element_type=jnp.float32)
    grad_act = (grad_fit * (1.0 - fit_hidden * fit_hidden)).astype(jnp.bfloat16)
    grad_descr = jnp.dot(grad_act, w_fit1.T, preferred_element_type=jnp.float32).reshape(blocks, embedding_width, -1)
    grad_tensor = jnp.einsum('bek,bck->bce', grad_descr, axis_part, precision=highest_precision)
    extra_grad = jnp.einsum('bek,bce->bck', grad_descr, descriptor_tensor, precision=highest_precision)
    grad_tensor = grad_tensor + jnp.pad(extra_grad, ((0, 0), (0, 0), (0, embedding_width - extra_grad.shape[2])))
    descriptor_product_gradient = grad_tensor.astype(jnp.bfloat16)
    environment_gradient = jnp.einsum('ohm,hdo->dhm', embedding_rows.astype(jnp.float32), descriptor_product_gradient.astype(jnp.float32), precision=highest_precision) / NEIGHBOUR_SLOTS
    embedding_gradient = jnp.einsum('zmj,mzr->rmj', environment_matrix.astype(jnp.float32), descriptor_product_gradient.astype(jnp.float32), precision=highest_precision).reshape(embedding_width, -1) / NEIGHBOUR_SLOTS
    grad_third = (embedding_gradient * (1.0 - tanh_third * tanh_third)).astype(jnp.bfloat16)
    half_width = embedding_width // 2
    grad_hidden2 = embedding_gradient[:half_width] + embedding_gradient[half_width:] + jnp.dot(w_embed3, grad_third, preferred_element_type=jnp.float32)
    grad_second = (grad_hidden2 * (1.0 - tanh_second * tanh_second)).astype(jnp.bfloat16)
    quarter = half_width // 2
    grad_hidden1 = grad_hidden2[:quarter] + grad_hidden2[quarter:] + jnp.dot(w_embed2, grad_second, preferred_element_type=jnp.float32)
    grad_smooth = jnp.dot(w_embed1, grad_hidden1 * (1.0 - hidden_first * hidden_first), precision=highest_precision).reshape(blocks, slot_count) + environment_gradient[0]
    radial = lax.optimization_barrier(jnp.sum(environment_gradient[1:] * displace, axis=0))
    factor = -grad_smooth / (radius * quad_dist) - 2.0 * radial / (quad_dist * quad_dist)
    pair_grad = live_mask[None] * (displace * factor[None] + environment_gradient[1:] / quad_dist[None])
    return (energy, pair_grad)

def evaluate(coords, neighbors, weights):
    atom_count = coords.shape[1]
    row_ids = jnp.arange(atom_count, dtype=jnp.int32)
    safe_index = jnp.maximum(neighbors, 0).astype(jnp.int32)
    live_mask = (neighbors >= 0).astype(jnp.float32)
    table_part = safe_index // BRICK
    anchor = (row_ids // BRICK)[:, None] + table_part - 1
    global_index = (anchor % N_BRICK * BRICK + safe_index % BRICK).astype(jnp.int32)
    shift_x = (table_part - 1).astype(jnp.float32)
    block_count = atom_count // ATOM_DEV

    def one_block(pieces):
        own_pos, table_index, offset, mask_rows = pieces
        neighbour_pos = jnp.take(coords, table_index, axis=1)
        displace = neighbour_pos - own_pos[:, :, None]
        displace = jnp.concatenate([displace[:1] + offset[None], displace[1:]], axis=0) * mask_rows[None]
        return pair_terms(displace, mask_rows, weights)
    own_blocks = coords.reshape(3, block_count, ATOM_DEV).transpose(1, 0, 2)
    energy, pair_grads = lax.map(one_block, (own_blocks, global_index.reshape(block_count, ATOM_DEV, -1), shift_x.reshape(block_count, ATOM_DEV, -1), live_mask.reshape(block_count, ATOM_DEV, -1)))
    pair_grads = pair_grads.transpose(1, 0, 2, 3).reshape(3, atom_count, -1)
    gathered = jnp.zeros((3, atom_count), jnp.float32).at[:, global_index].add(pair_grads)
    return (energy.reshape(-1), lax.optimization_barrier(jnp.sum(pair_grads, axis=2)) - gathered)

def reference(positions, velocities, forces_in, neighbors, w_embed1, b_embed1, w_embed2, b_embed2, w_embed3, b_embed3, w_fit1, b_fit1, w_fit2, b_fit2, w_out):
    weights = (w_embed1, b_embed1, w_embed2, b_embed2, w_embed3, b_embed3, w_fit1, b_fit1, w_fit2, b_fit2, w_out)
    coords = positions
    speed = velocities
    force_now = forces_in
    energy = jnp.zeros((positions.shape[1],), jnp.float32)
    for md_step in range(STEPS):
        speed = speed + kick_scale * force_now
        coords = coords + time_step * speed
        energy, force_now = evaluate(coords, neighbors, weights)
        speed = speed + kick_scale * force_now
    return (coords, speed, energy, force_now)
```

```python
import functools

import jax
import jax.numpy as jnp
from jax import lax
from jax.experimental import pallas as pl
from jax.experimental.pallas import tpu as pltpu
from jax.sharding import PartitionSpec as P

STEPS = 2

kick_scale = 0.25
time_step = 0.05
LANES = 128
f32 = jnp.float32
bf16 = jnp.bfloat16
NN = (((1,), (0,)), ((), ()))
NT = (((1,), (1,)), ((), ()))
TN = (((0,), (0,)), ((), ()))


def mm(a, b, dims=NN):
    return lax.dot_general(a, b, dims, preferred_element_type=f32)


def split2(x):
    high = x.astype(bf16).astype(f32)
    return high, x - high


def eval_kernel(
    rank_ref,
    before_ref,
    brick_ref,
    after_ref,
    own_ref,
    nbr_ref,
    w1_ref,
    b1_ref,
    w2t_ref,
    w2_ref,
    b2_ref,
    w3t_ref,
    w3_ref,
    b3_ref,
    f1_ref,
    c1_ref,
    f2_ref,
    c2_ref,
    out_ref,
    energy_ref,
    to_before_ref,
    to_brick_ref,
    to_after_ref,
    s_s,
    r_s,
    t_s,
    d_s,
    h1_s,
    u2_s,
    u3_s,
    g_s,
    z_s,
    dr_s,
    hi_s,
    lo_s,
    gr_s,
    des_s,
):
    atoms, slots = nbr_ref.shape
    brick_len = brick_ref.shape[1]
    per = brick_len // LANES
    e1 = w1_ref.shape[0]
    e2 = w2_ref.shape[1]
    e3 = w3_ref.shape[1]
    m2 = f1_ref.shape[0] // e3
    inv_slots = 1.0 / slots
    pairs = atoms // 2

    nbr = nbr_ref[...]
    live = nbr >= 0
    mask = jnp.where(live, 1.0, 0.0).astype(f32)
    index = jnp.maximum(nbr, 0)
    low = index & (LANES - 1)
    high = lax.shift_right_logical(index, 7)
    sub = lax.broadcasted_iota(jnp.int32, (atoms, slots), 0)
    coords = [jnp.zeros((atoms, slots), f32)] * 3
    for part, table in enumerate((before_ref, brick_ref, after_ref)):
        for chunk in range(per):
            hit = high == part * per + chunk
            for c in range(3):
                row = table[c : c + 1, chunk * LANES : (chunk + 1) * LANES]
                found = jnp.take_along_axis(
                    jnp.broadcast_to(row, (atoms, LANES)), low, axis=1, mode="promise_in_bounds"
                )
                coords[c] = jnp.where(hit, found, coords[c])
    shift = (
        jnp.where(high >= per, 1.0, 0.0) + jnp.where(high >= 2 * per, 1.0, 0.0) - 1.0
    ).astype(f32)
    disp = []
    for c in range(3):
        row = own_ref[c : c + 1, :]
        mine = jnp.take_along_axis(
            jnp.broadcast_to(row, (atoms, LANES)), sub, axis=1, mode="promise_in_bounds"
        )
        delta = coords[c] - mine
        if c == 0:
            delta = delta + shift
        disp.append(delta * mask)
    quad = disp[0] * disp[0] + disp[1] * disp[1] + disp[2] * disp[2] + 0.25
    radius = jnp.sqrt(quad)
    smooth = mask / radius
    inv_quad = 1.0 / quad
    s_s[...] = smooth
    r_s[pl.ds(0, atoms, stride=4), :] = smooth
    for c in range(3):
        r_s[pl.ds(c + 1, atoms, stride=4), :] = disp[c] * inv_quad
    hi_s[...] = high
    lo_s[...] = low

    w1 = jnp.broadcast_to(w1_ref[...], (e1, LANES))
    b1 = jnp.broadcast_to(b1_ref[...], (e1, LANES))
    w1 = jnp.concatenate([w1, w1], axis=1)
    b1 = jnp.concatenate([b1, b1], axis=1)
    row8 = lax.broadcasted_iota(jnp.int32, (8, LANES), 0)

    def both(value):
        left = jnp.where(row8 < 4, value, 0.0)
        right = jnp.where(row8 >= 4, value, 0.0)
        return jnp.concatenate([left, right], axis=1)

    def forward(p, carry):
        base = pl.multiple_of(p * 8, 8)
        s_row = jnp.concatenate(
            [
                jnp.broadcast_to(s_s[pl.ds(2 * p, 1), :], (e1, LANES)),
                jnp.broadcast_to(s_s[pl.ds(2 * p + 1, 1), :], (e1, LANES)),
            ],
            axis=1,
        )
        h1 = jnp.tanh(w1 * s_row + b1)
        t2 = jnp.tanh(mm(w2t_ref[...], h1.astype(bf16)) + b2_ref[...])
        h2 = jnp.concatenate([h1, h1], axis=0) + t2
        t3 = jnp.tanh(mm(w3t_ref[...], h2.astype(bf16)) + b3_ref[...])
        g = (jnp.concatenate([h2, h2], axis=0) + t3).astype(bf16)
        h1_s[p] = h1
        u2_s[p] = 1.0 - t2 * t2
        u3_s[p] = 1.0 - t3 * t3
        g_s[p] = g
        r2 = both(r_s[pl.ds(base, 8), :]).astype(bf16)
        t_s[pl.ds(base, 8), :] = mm(r2, g, NT) * inv_slots
        return carry

    lax.fori_loop(0, pairs, forward, 0)

    tens = [t_s[pl.ds(c, atoms, stride=4), :] for c in range(4)]
    for k in range(m2):
        total = tens[0] * jnp.broadcast_to(tens[0][:, k : k + 1], (atoms, e3))
        for c in range(1, 4):
            total = total + tens[c] * jnp.broadcast_to(tens[c][:, k : k + 1], (atoms, e3))
        des_s[:, k * e3 : (k + 1) * e3] = total.astype(bf16)
    wide = out_ref[...]
    y1 = jnp.tanh(mm(des_s[...], f1_ref[...]) + c1_ref[...])
    t4 = jnp.tanh(mm(y1.astype(bf16), f2_ref[...]) + c2_ref[...])
    energy_ref[...] = lax.dot_general(
        wide, y1 + t4, NT, precision=lax.Precision.HIGHEST, preferred_element_type=f32
    )
    dz2 = (wide * (1.0 - t4 * t4)).astype(bf16)
    dy1 = wide + mm(dz2, f2_ref[...], NT)
    dz1 = (dy1 * (1.0 - y1 * y1)).astype(bf16)
    lane = lax.broadcasted_iota(jnp.int32, (atoms, e3), 1)
    grads = [jnp.zeros((atoms, e3), f32)] * 4
    for k in range(m2):
        dd = mm(dz1, f1_ref[k * e3 : (k + 1) * e3, :], NT)
        for c in range(4):
            other = jnp.sum(dd * tens[c], axis=1, keepdims=True)
            grads[c] = (
                grads[c]
                + dd * jnp.broadcast_to(tens[c][:, k : k + 1], (atoms, e3))
                + jnp.where(lane == k, other, 0.0)
            )
    for c in range(4):
        d_s[pl.ds(c, atoms, stride=4), :] = grads[c].astype(bf16).astype(f32) * inv_slots

    def backward(p, carry):
        base = pl.multiple_of(p * 8, 8)
        dt = d_s[pl.ds(base, 8), :].astype(bf16)
        r2 = both(r_s[pl.ds(base, 8), :]).astype(bf16)
        dr = mm(dt, g_s[p])
        dr_s[pl.ds(base, 8), :] = jnp.where(row8 < 4, dr[:, :LANES], dr[:, LANES:])
        dg = mm(dt, r2, TN)
        da3 = (dg * u3_s[p]).astype(bf16)
        dh2 = dg[: e3 // 2] + dg[e3 // 2 :] + mm(w3_ref[...], da3)
        da2 = (dh2 * u2_s[p]).astype(bf16)
        dh1 = dh2[: e2 // 2] + dh2[e2 // 2 :] + mm(w2_ref[...], da2)
        h1 = h1_s[p]
        part = dh1 * (1.0 - h1 * h1) * w1
        z = part[0:8]
        for i in range(1, e1 // 8):
            z = z + part[8 * i : 8 * i + 8]
        wide_base = pl.multiple_of(p * 16, 16)
        z_s[pl.ds(wide_base, 8), :] = z[:, :LANES]
        z_s[pl.ds(wide_base + 8, 8), :] = z[:, LANES:]
        return carry

    lax.fori_loop(0, pairs, backward, 0)

    ds = dr_s[pl.ds(0, atoms, stride=4), :]
    for i in range(8):
        ds = ds + z_s[pl.ds(i, atoms, stride=8), :]
    drs = [dr_s[pl.ds(c + 1, atoms, stride=4), :] for c in range(3)]
    radial = drs[0] * disp[0] + drs[1] * disp[1] + drs[2] * disp[2]
    factor = -ds / (radius * quad) - 2.0 * radial * (inv_quad * inv_quad)
    ones = jnp.ones((8, LANES), bf16)
    zero = jnp.zeros((atoms, LANES), f32)
    sums = []
    for c in range(3):
        pull = mask * (disp[c] * factor + drs[c] * inv_quad)
        upper, lower = split2(pull)
        gr_s[pl.ds(c, atoms, stride=8), :] = upper
        gr_s[pl.ds(c + 3, atoms, stride=8), :] = lower
        both_parts = mm(ones, upper.astype(bf16), NT) + mm(ones, lower.astype(bf16), NT)
        sums.append(both_parts[0:1])
    gr_s[pl.ds(6, atoms, stride=8), :] = zero
    gr_s[pl.ds(7, atoms, stride=8), :] = zero
    mine = jnp.concatenate(sums, axis=0)

    place = lax.broadcasted_iota(jnp.int32, (LANES, LANES), 0)
    chunks = 3 * per

    def scatter(p, total):
        rows = []
        hots = []
        for i in range(2):
            atom = 2 * p + i
            values = gr_s[pl.ds(pl.multiple_of(atom * 8, 8), 8), :]
            upper = jnp.broadcast_to(hi_s[pl.ds(atom, 1), :], (8, LANES))
            lower = jnp.broadcast_to(lo_s[pl.ds(atom, 1), :], (LANES, LANES))
            rows.append(
                jnp.concatenate(
                    [jnp.where(upper == a, values, 0.0) for a in range(chunks)], axis=0
                )
            )
            hots.append(jnp.where(lower == place, 1.0, 0.0).astype(bf16))
        lhs = jnp.concatenate(rows, axis=1).astype(bf16)
        return total + mm(lhs, jnp.concatenate(hots, axis=1), NT)

    total = lax.fori_loop(0, pairs, scatter, jnp.zeros((8 * chunks, LANES), f32))
    rank = rank_ref[0]
    spot = lax.broadcasted_iota(jnp.int32, (3, brick_len), 1) // atoms
    placed = jnp.where(
        spot == rank, jnp.concatenate([mine] * (brick_len // atoms), axis=1), 0.0
    )
    for part, target in enumerate((to_before_ref, to_brick_ref, to_after_ref)):
        pieces = []
        for chunk in range(per):
            at = 8 * (part * per + chunk)
            pieces.append(total[at : at + 3] + total[at + 3 : at + 6])
        whole = -jnp.concatenate(pieces, axis=1)
        target[...] = whole + placed if part == 1 else whole


def prepare(weights, lanes):
    w1, b1, w2, b2, w3, b3, f1, c1, f2, c2, out = weights
    e3 = w3.shape[1]
    fit = out.shape[0]
    pad = -fit % LANES
    m2 = f1.shape[0] // e3
    f1 = jnp.pad(f1.reshape(e3, m2, fit).transpose(1, 0, 2), ((0, 0), (0, 0), (0, pad)))
    return (
        w1[:, None],
        b1[:, None],
        w2.T,
        w2,
        b2[:, None],
        w3.T,
        w3,
        b3[:, None],
        f1.reshape(m2 * e3, fit + pad),
        jnp.pad(c1, (0, pad))[None],
        jnp.pad(f2, ((0, pad), (0, pad))),
        jnp.pad(c2, (0, pad))[None],
        jnp.pad(out, (0, pad))[None],
    )


def evaluate(rank, before, brick, after, own, neighbors, prepared):
    atoms, slots = neighbors.shape
    brick_len = brick.shape[1]
    e1 = prepared[0].shape[0]
    e2 = prepared[3].shape[1]
    e3 = prepared[6].shape[1]
    pairs = atoms // 2
    wide = 2 * slots
    own = jnp.concatenate([own, own], axis=1)[:, :LANES]
    vmem = pl.BlockSpec(memory_space=pltpu.VMEM)
    piece = jax.ShapeDtypeStruct((3, brick_len), f32)
    return pl.pallas_call(
        eval_kernel,
        out_shape=(jax.ShapeDtypeStruct((1, atoms), f32), piece, piece, piece),
        in_specs=[pl.BlockSpec(memory_space=pltpu.SMEM)] + [vmem] * (5 + len(prepared)),
        out_specs=[vmem] * 4,
        scratch_shapes=[
            pltpu.VMEM((atoms, slots), f32),
            pltpu.VMEM((4 * atoms, slots), f32),
            pltpu.VMEM((4 * atoms, e3), f32),
            pltpu.VMEM((4 * atoms, e3), f32),
            pltpu.VMEM((pairs, e1, wide), f32),
            pltpu.VMEM((pairs, e2, wide), f32),
            pltpu.VMEM((pairs, e3, wide), f32),
            pltpu.VMEM((pairs, e3, wide), bf16),
            pltpu.VMEM((8 * atoms, slots), f32),
            pltpu.VMEM((4 * atoms, slots), f32),
            pltpu.VMEM((atoms, slots), jnp.int32),
            pltpu.VMEM((atoms, slots), jnp.int32),
            pltpu.VMEM((8 * atoms, slots), f32),
            pltpu.VMEM((atoms, prepared[8].shape[0]), bf16),
        ],
        compiler_params=pltpu.CompilerParams(vmem_limit_bytes=40 * 1024 * 1024),
        name="evaluate",
    )(rank, before, brick, after, own, neighbors, *prepared)


def ring(size, step):
    return [(i, (i + step) % size) for i in range(size)]


def flip(size, bit):
    return [(i, i ^ bit) for i in range(size)]


def gather_help(value):
    size = lax.axis_size("help")
    rank = lax.axis_index("help")
    if size & (size - 1):
        return lax.all_gather(value, "help", axis=1, tiled=True)
    bit = 1
    while bit < size:
        other = lax.ppermute(value, "help", flip(size, bit))
        upper = (rank & bit) != 0
        value = jnp.where(
            upper,
            jnp.concatenate([other, value], axis=1),
            jnp.concatenate([value, other], axis=1),
        )
        bit *= 2
    return value


def sum_help(value):
    size = lax.axis_size("help")
    if size & (size - 1):
        return lax.psum(value, "help")
    bit = 1
    while bit < size:
        value = value + lax.ppermute(value, "help", flip(size, bit))
        bit *= 2
    return value


def exchange(up, down):
    size = lax.axis_size("brick")
    return lax.ppermute(up, "brick", ring(size, 1)), lax.ppermute(down, "brick", ring(size, -1))


def local(positions, velocities, forces_in, neighbors, *weights):
    prepared = prepare(weights, LANES)
    atoms = positions.shape[1]
    rank = lax.axis_index("help")
    ranks = rank.reshape(1).astype(jnp.int32)
    at = rank * atoms
    speed = velocities + kick_scale * forces_in
    coords = positions + time_step * speed
    state = gather_help(jnp.concatenate([coords, speed], axis=0))
    brick_pos, brick_speed = state[:3], state[3:]
    own = coords
    for md_step in range(STEPS):
        before, after = exchange(brick_pos, brick_pos)
        energy, to_before, to_brick, to_after = evaluate(
            ranks, before, brick_pos, after, own, neighbors, prepared
        )
        from_before, from_after = exchange(to_after, to_before)
        force = sum_help(to_brick + from_before + from_after)
        brick_speed = brick_speed + kick_scale * force
        if md_step + 1 < STEPS:
            brick_speed = brick_speed + kick_scale * force
            brick_pos = brick_pos + time_step * brick_speed
            own = lax.dynamic_slice_in_dim(brick_pos, at, atoms, axis=1)
    out = lax.dynamic_slice_in_dim(
        jnp.concatenate([brick_speed, force], axis=0), at, atoms, axis=1
    )
    return (own, out[:3], energy.reshape(atoms), out[3:])


def solution(mesh):
    spread = ("brick", "help")
    cols = P(None, spread)
    return jax.shard_map(
        local,
        mesh=mesh,
        in_specs=(cols, cols, cols, P(spread, None)) + (P(),) * 11,
        out_specs=(cols, cols, P(spread), cols),
        check_vma=False,
    )
```

```python
import functools

import jax
import jax.numpy as jnp
from jax import lax
from jax.experimental import pallas as pl
from jax.experimental.pallas import tpu as pltpu
from jax.sharding import PartitionSpec as P

STEPS = 2

kick_scale = 0.25
time_step = 0.05
LANES = 128
GROUP = 4
f32 = jnp.float32
bf16 = jnp.bfloat16
NN = (((1,), (0,)), ((), ()))
NT = (((1,), (1,)), ((), ()))
TN = (((0,), (0,)), ((), ()))


def mm(a, b, dims=NN):
    return lax.dot_general(a, b, dims, preferred_element_type=f32)


def split2(x):
    high = x.astype(bf16).astype(f32)
    return high, x - high


def eval_kernel(
    rank_ref,
    before_ref,
    brick_ref,
    after_ref,
    own_ref,
    nbr_ref,
    w1_ref,
    b1_ref,
    w2t_ref,
    w2_ref,
    b2_ref,
    w3t_ref,
    w3_ref,
    b3_ref,
    f1_ref,
    c1_ref,
    f2_ref,
    c2_ref,
    out_ref,
    energy_ref,
    to_before_ref,
    to_brick_ref,
    to_after_ref,
    s_s,
    r_s,
    t_s,
    d_s,
    h1_s,
    h2_s,
    u2_s,
    u3_s,
    g_s,
    da3_s,
    dg_s,
    da2_s,
    dh2_s,
    z_s,
    dr_s,
    hi_s,
    lo_s,
    gr_s,
    des_s,
):
    atoms, slots = nbr_ref.shape
    brick_len = brick_ref.shape[1]
    per = brick_len // LANES
    e1 = w1_ref.shape[0]
    e2 = w2_ref.shape[1]
    e3 = w3_ref.shape[1]
    m2 = f1_ref.shape[0] // e3
    inv_slots = 1.0 / slots
    pairs = atoms // 2

    nbr = nbr_ref[...]
    live = nbr >= 0
    mask = jnp.where(live, 1.0, 0.0).astype(f32)
    index = jnp.maximum(nbr, 0)
    low = index & (LANES - 1)
    high = lax.shift_right_logical(index, 7)
    sub = lax.broadcasted_iota(jnp.int32, (atoms, slots), 0)
    coords = [jnp.zeros((atoms, slots), f32)] * 3
    for part, table in enumerate((before_ref, brick_ref, after_ref)):
        for chunk in range(per):
            hit = high == part * per + chunk
            for c in range(3):
                row = table[c : c + 1, chunk * LANES : (chunk + 1) * LANES]
                found = jnp.take_along_axis(
                    jnp.broadcast_to(row, (atoms, LANES)), low, axis=1, mode="promise_in_bounds"
                )
                coords[c] = jnp.where(hit, found, coords[c])
    shift = (
        jnp.where(high >= per, 1.0, 0.0) + jnp.where(high >= 2 * per, 1.0, 0.0) - 1.0
    ).astype(f32)
    disp = []
    for c in range(3):
        row = own_ref[c : c + 1, :]
        mine = jnp.take_along_axis(
            jnp.broadcast_to(row, (atoms, LANES)), sub, axis=1, mode="promise_in_bounds"
        )
        delta = coords[c] - mine
        if c == 0:
            delta = delta + shift
        disp.append(delta * mask)
    quad = disp[0] * disp[0] + disp[1] * disp[1] + disp[2] * disp[2] + 0.25
    radius = jnp.sqrt(quad)
    smooth = mask / radius
    inv_quad = 1.0 / quad
    s_s[...] = smooth
    r_s[pl.ds(0, atoms, stride=4), :] = smooth
    for c in range(3):
        r_s[pl.ds(c + 1, atoms, stride=4), :] = disp[c] * inv_quad
    hi_s[...] = high
    lo_s[...] = low

    width = GROUP * slots
    groups = atoms // GROUP
    w1 = jnp.broadcast_to(w1_ref[...], (e1, LANES))
    b1 = jnp.broadcast_to(b1_ref[...], (e1, LANES))
    row16 = lax.broadcasted_iota(jnp.int32, (4 * GROUP, LANES), 0) // 4

    def spread(value):
        return jnp.concatenate(
            [jnp.where(row16 == a, value, 0.0) for a in range(GROUP)], axis=1
        ).astype(bf16)

    def collect(value):
        total = value[:, :LANES]
        for a in range(1, GROUP):
            total = jnp.where(row16 == a, value[:, a * LANES : (a + 1) * LANES], total)
        return total

    def at(step, lag):
        return jnp.clip(step - lag, 0, groups - 1)

    def rows16(group):
        return pl.ds(pl.multiple_of(group * 4 * GROUP, 4 * GROUP), 4 * GROUP)

    def forward(step, carry):
        j = at(step, 3)
        t_s[rows16(j), :] = mm(spread(r_s[rows16(j), :]), g_s[j], NT) * inv_slots

        j = at(step, 2)
        h2 = h2_s[j]
        t3 = jnp.tanh(mm(w3t_ref[...], h2.astype(bf16)) + b3_ref[...])
        g_s[j] = (jnp.concatenate([h2, h2], axis=0) + t3).astype(bf16)
        u3_s[j] = 1.0 - t3 * t3

        j = at(step, 1)
        h1 = h1_s[j]
        t2 = jnp.tanh(mm(w2t_ref[...], h1.astype(bf16)) + b2_ref[...])
        h2_s[j] = jnp.concatenate([h1, h1], axis=0) + t2
        u2_s[j] = 1.0 - t2 * t2

        j = at(step, 0)
        for a in range(GROUP):
            s_row = jnp.broadcast_to(s_s[pl.ds(GROUP * j + a, 1), :], (e1, LANES))
            h1_s[j, :, a * LANES : (a + 1) * LANES] = jnp.tanh(w1 * s_row + b1)
        return carry

    lax.fori_loop(0, groups + 3, forward, 0)

    tens = [t_s[pl.ds(c, atoms, stride=4), :] for c in range(4)]
    for k in range(m2):
        total = tens[0] * jnp.broadcast_to(tens[0][:, k : k + 1], (atoms, e3))
        for c in range(1, 4):
            total = total + tens[c] * jnp.broadcast_to(tens[c][:, k : k + 1], (atoms, e3))
        des_s[:, k * e3 : (k + 1) * e3] = total.astype(bf16)
    wide = out_ref[...]
    y1 = jnp.tanh(mm(des_s[...], f1_ref[...]) + c1_ref[...])
    t4 = jnp.tanh(mm(y1.astype(bf16), f2_ref[...]) + c2_ref[...])
    energy_ref[...] = lax.dot_general(
        wide, y1 + t4, NT, precision=lax.Precision.HIGHEST, preferred_element_type=f32
    )
    dz2 = (wide * (1.0 - t4 * t4)).astype(bf16)
    dy1 = wide + mm(dz2, f2_ref[...], NT)
    dz1 = (dy1 * (1.0 - y1 * y1)).astype(bf16)
    lane = lax.broadcasted_iota(jnp.int32, (atoms, e3), 1)
    grads = [jnp.zeros((atoms, e3), f32)] * 4
    for k in range(m2):
        dd = mm(dz1, f1_ref[k * e3 : (k + 1) * e3, :], NT)
        for c in range(4):
            other = jnp.sum(dd * tens[c], axis=1, keepdims=True)
            grads[c] = (
                grads[c]
                + dd * jnp.broadcast_to(tens[c][:, k : k + 1], (atoms, e3))
                + jnp.where(lane == k, other, 0.0)
            )
    for c in range(4):
        d_s[pl.ds(c, atoms, stride=4), :] = grads[c].astype(bf16).astype(f32) * inv_slots

    def backward(step, carry):
        j = at(step, 2)
        dh1 = dh2_s[j] + mm(w2_ref[...], da2_s[j])
        h1 = h1_s[j]
        part = dh1 * (1.0 - h1 * h1)
        for a in range(GROUP):
            z = None
            for i in range(0, e1, 8):
                term = part[i : i + 8, a * LANES : (a + 1) * LANES] * w1[i : i + 8]
                z = term if z is None else z + term
            z_s[pl.ds(pl.multiple_of((GROUP * j + a) * 8, 8), 8), :] = z

        j = at(step, 1)
        dh2 = dg_s[j] + mm(w3_ref[...], da3_s[j])
        da2_s[j] = (dh2 * u2_s[j]).astype(bf16)
        dh2_s[j] = dh2[: e2 // 2] + dh2[e2 // 2 :]

        j = at(step, 0)
        dt = d_s[rows16(j), :].astype(bf16)
        dr_s[rows16(j), :] = collect(mm(dt, g_s[j]))
        dg = mm(dt, spread(r_s[rows16(j), :]), TN)
        da3_s[j] = (dg * u3_s[j]).astype(bf16)
        dg_s[j] = dg[: e3 // 2] + dg[e3 // 2 :]
        return carry

    lax.fori_loop(0, groups + 2, backward, 0)

    ds = dr_s[pl.ds(0, atoms, stride=4), :]
    for i in range(8):
        ds = ds + z_s[pl.ds(i, atoms, stride=8), :]
    drs = [dr_s[pl.ds(c + 1, atoms, stride=4), :] for c in range(3)]
    radial = drs[0] * disp[0] + drs[1] * disp[1] + drs[2] * disp[2]
    factor = -ds / (radius * quad) - 2.0 * radial * (inv_quad * inv_quad)
    ones = jnp.ones((8, LANES), bf16)
    zero = jnp.zeros((atoms, LANES), f32)
    sums = []
    for c in range(3):
        pull = mask * (disp[c] * factor + drs[c] * inv_quad)
        upper, lower = split2(pull)
        gr_s[pl.ds(c, atoms, stride=8), :] = upper
        gr_s[pl.ds(c + 3, atoms, stride=8), :] = lower
        both_parts = mm(ones, upper.astype(bf16), NT) + mm(ones, lower.astype(bf16), NT)
        sums.append(both_parts[0:1])
    gr_s[pl.ds(6, atoms, stride=8), :] = zero
    gr_s[pl.ds(7, atoms, stride=8), :] = zero
    mine = jnp.concatenate(sums, axis=0)

    place = lax.broadcasted_iota(jnp.int32, (LANES, LANES), 0)
    chunks = 3 * per

    def scatter(p, total):
        rows = []
        hots = []
        for i in range(2):
            atom = 2 * p + i
            values = gr_s[pl.ds(pl.multiple_of(atom * 8, 8), 8), :]
            upper = jnp.broadcast_to(hi_s[pl.ds(atom, 1), :], (8, LANES))
            lower = jnp.broadcast_to(lo_s[pl.ds(atom, 1), :], (LANES, LANES))
            rows.append(
                jnp.concatenate(
                    [jnp.where(upper == a, values, 0.0) for a in range(chunks)], axis=0
                )
            )
            hots.append(jnp.where(lower == place, 1.0, 0.0).astype(bf16))
        lhs = jnp.concatenate(rows, axis=1).astype(bf16)
        return total + mm(lhs, jnp.concatenate(hots, axis=1), NT)

    total = lax.fori_loop(0, pairs, scatter, jnp.zeros((8 * chunks, LANES), f32), unroll=4)
    rank = rank_ref[0]
    spot = lax.broadcasted_iota(jnp.int32, (3, brick_len), 1) // atoms
    placed = jnp.where(
        spot == rank, jnp.concatenate([mine] * (brick_len // atoms), axis=1), 0.0
    )
    for part, target in enumerate((to_before_ref, to_brick_ref, to_after_ref)):
        pieces = []
        for chunk in range(per):
            at = 8 * (part * per + chunk)
            pieces.append(total[at : at + 3] + total[at + 3 : at + 6])
        whole = -jnp.concatenate(pieces, axis=1)
        target[...] = whole + placed if part == 1 else whole


def prepare(weights, lanes):
    w1, b1, w2, b2, w3, b3, f1, c1, f2, c2, out = weights
    e3 = w3.shape[1]
    fit = out.shape[0]
    pad = -fit % LANES
    m2 = f1.shape[0] // e3
    f1 = jnp.pad(f1.reshape(e3, m2, fit).transpose(1, 0, 2), ((0, 0), (0, 0), (0, pad)))
    return (
        w1[:, None],
        b1[:, None],
        w2.T,
        w2,
        b2[:, None],
        w3.T,
        w3,
        b3[:, None],
        f1.reshape(m2 * e3, fit + pad),
        jnp.pad(c1, (0, pad))[None],
        jnp.pad(f2, ((0, pad), (0, pad))),
        jnp.pad(c2, (0, pad))[None],
        jnp.pad(out, (0, pad))[None],
    )


def evaluate(rank, before, brick, after, own, neighbors, prepared):
    atoms, slots = neighbors.shape
    brick_len = brick.shape[1]
    e1 = prepared[0].shape[0]
    e2 = prepared[3].shape[1]
    e3 = prepared[6].shape[1]
    groups = atoms // GROUP
    wide = GROUP * slots
    own = jnp.concatenate([own, own], axis=1)[:, :LANES]
    vmem = pl.BlockSpec(memory_space=pltpu.VMEM)
    piece = jax.ShapeDtypeStruct((3, brick_len), f32)
    return pl.pallas_call(
        eval_kernel,
        out_shape=(jax.ShapeDtypeStruct((1, atoms), f32), piece, piece, piece),
        in_specs=[pl.BlockSpec(memory_space=pltpu.SMEM)] + [vmem] * (5 + len(prepared)),
        out_specs=[vmem] * 4,
        scratch_shapes=[
            pltpu.VMEM((atoms, slots), f32),
            pltpu.VMEM((4 * atoms, slots), f32),
            pltpu.VMEM((4 * atoms, e3), f32),
            pltpu.VMEM((4 * atoms, e3), f32),
            pltpu.VMEM((groups, e1, wide), f32),
            pltpu.VMEM((groups, e2, wide), f32),
            pltpu.VMEM((groups, e2, wide), f32),
            pltpu.VMEM((groups, e3, wide), f32),
            pltpu.VMEM((groups, e3, wide), bf16),
            pltpu.VMEM((groups, e3, wide), bf16),
            pltpu.VMEM((groups, e2, wide), f32),
            pltpu.VMEM((groups, e2, wide), bf16),
            pltpu.VMEM((groups, e1, wide), f32),
            pltpu.VMEM((8 * atoms, slots), f32),
            pltpu.VMEM((4 * atoms, slots), f32),
            pltpu.VMEM((atoms, slots), jnp.int32),
            pltpu.VMEM((atoms, slots), jnp.int32),
            pltpu.VMEM((8 * atoms, slots), f32),
            pltpu.VMEM((atoms, prepared[8].shape[0]), bf16),
        ],
        compiler_params=pltpu.CompilerParams(vmem_limit_bytes=40 * 1024 * 1024),
        name="evaluate",
    )(rank, before, brick, after, own, neighbors, *prepared)


def ring(size, step):
    return [(i, (i + step) % size) for i in range(size)]


def flip(size, bit):
    return [(i, i ^ bit) for i in range(size)]


def gather_help(value):
    size = lax.axis_size("help")
    rank = lax.axis_index("help")
    if size & (size - 1):
        return lax.all_gather(value, "help", axis=1, tiled=True)
    bit = 1
    while bit < size:
        other = lax.ppermute(value, "help", flip(size, bit))
        upper = (rank & bit) != 0
        value = jnp.where(
            upper,
            jnp.concatenate([other, value], axis=1),
            jnp.concatenate([value, other], axis=1),
        )
        bit *= 2
    return value


def sum_help(value):
    size = lax.axis_size("help")
    if size & (size - 1):
        return lax.psum(value, "help")
    bit = 1
    while bit < size:
        value = value + lax.ppermute(value, "help", flip(size, bit))
        bit *= 2
    return value


def exchange(up, down):
    size = lax.axis_size("brick")
    return lax.ppermute(up, "brick", ring(size, 1)), lax.ppermute(down, "brick", ring(size, -1))


def local(positions, velocities, forces_in, neighbors, *weights):
    prepared = prepare(weights, LANES)
    atoms = positions.shape[1]
    rank = lax.axis_index("help")
    ranks = rank.reshape(1).astype(jnp.int32)
    at = rank * atoms
    speed = velocities + kick_scale * forces_in
    coords = positions + time_step * speed
    state = gather_help(jnp.concatenate([coords, speed], axis=0))
    brick_pos, brick_speed = state[:3], state[3:]
    own = coords
    for md_step in range(STEPS):
        before, after = exchange(brick_pos, brick_pos)
        energy, to_before, to_brick, to_after = evaluate(
            ranks, before, brick_pos, after, own, neighbors, prepared
        )
        from_before, from_after = exchange(to_after, to_before)
        force = sum_help(to_brick + from_before + from_after)
        brick_speed = brick_speed + kick_scale * force
        if md_step + 1 < STEPS:
            brick_speed = brick_speed + kick_scale * force
            brick_pos = brick_pos + time_step * brick_speed
            own = lax.dynamic_slice_in_dim(brick_pos, at, atoms, axis=1)
    out = lax.dynamic_slice_in_dim(
        jnp.concatenate([brick_speed, force], axis=0), at, atoms, axis=1
    )
    return (own, out[:3], energy.reshape(atoms), out[3:])


def solution(mesh):
    spread = ("brick", "help")
    cols = P(None, spread)
    return jax.shard_map(
        local,
        mesh=mesh,
        in_specs=(cols, cols, cols, P(spread, None)) + (P(),) * 11,
        out_specs=(cols, cols, P(spread), cols),
        check_vma=False,
    )
```

```python
import functools

import jax
import jax.numpy as jnp
from jax import lax
from jax.experimental import pallas as pl
from jax.experimental.pallas import tpu as pltpu
from jax.sharding import PartitionSpec as P

STEPS = 2

kick_scale = 0.25
time_step = 0.05
LANES = 128
PAIRS = 4
GROUP = 2 * PAIRS
f32 = jnp.float32
bf16 = jnp.bfloat16
NN = (((1,), (0,)), ((), ()))
NT = (((1,), (1,)), ((), ()))
TN = (((0,), (0,)), ((), ()))


def mm(a, b, dims=NN):
    return lax.dot_general(a, b, dims, preferred_element_type=f32)


def split2(x):
    high = x.astype(bf16).astype(f32)
    return high, x - high


def eval_kernel(
    rank_ref,
    before_ref,
    brick_ref,
    after_ref,
    own_ref,
    low_ref,
    high_ref,
    w1_ref,
    b1_ref,
    w2t_ref,
    w2_ref,
    b2_ref,
    w3t_ref,
    w3_ref,
    b3_ref,
    f1_ref,
    c1_ref,
    f2_ref,
    c2_ref,
    out_ref,
    energy_ref,
    to_before_ref,
    to_brick_ref,
    to_after_ref,
    s_s,
    r_s,
    t_s,
    d_s,
    h1_s,
    h2_s,
    u2_s,
    u3_s,
    g_s,
    da3_s,
    dg_s,
    da2_s,
    dh2_s,
    z_s,
    dr_s,
    gr_s,
    des_s,
):
    atoms, slots = low_ref.shape
    brick_len = brick_ref.shape[1]
    per = brick_len // LANES
    e1 = w1_ref.shape[0]
    e2 = b2_ref.shape[0] // PAIRS
    e3 = b3_ref.shape[0] // PAIRS
    m2 = f1_ref.shape[0] // e3
    inv_slots = 1.0 / slots
    pairs = atoms // 2

    low = low_ref[...]
    high = high_ref[...]
    mask = jnp.where(high >= 0, 1.0, 0.0).astype(f32)
    sub = lax.broadcasted_iota(jnp.int32, (atoms, slots), 0)
    coords = [jnp.zeros((atoms, slots), f32)] * 3
    for part, table in enumerate((before_ref, brick_ref, after_ref)):
        for chunk in range(per):
            hit = high == part * per + chunk
            for c in range(3):
                row = table[c : c + 1, chunk * LANES : (chunk + 1) * LANES]
                found = jnp.take_along_axis(
                    jnp.broadcast_to(row, (atoms, LANES)), low, axis=1, mode="promise_in_bounds"
                )
                coords[c] = jnp.where(hit, found, coords[c])
    shift = (
        jnp.where(high >= per, 1.0, 0.0) + jnp.where(high >= 2 * per, 1.0, 0.0) - 1.0
    ).astype(f32)
    disp = []
    for c in range(3):
        row = own_ref[c : c + 1, :]
        mine = jnp.take_along_axis(
            jnp.broadcast_to(row, (atoms, LANES)), sub, axis=1, mode="promise_in_bounds"
        )
        delta = coords[c] - mine
        if c == 0:
            delta = delta + shift
        disp.append(delta * mask)
    quad = disp[0] * disp[0] + disp[1] * disp[1] + disp[2] * disp[2] + 0.25
    radius = jnp.sqrt(quad)
    smooth = mask / radius
    inv_quad = 1.0 / quad
    s_s[...] = smooth
    r_s[pl.ds(0, atoms, stride=4), :] = smooth
    for c in range(3):
        r_s[pl.ds(c + 1, atoms, stride=4), :] = disp[c] * inv_quad

    groups = atoms // GROUP
    wide = 2 * slots
    half = 2 * e3
    w1 = w1_ref[...]
    b1 = b1_ref[...]
    row16 = lax.broadcasted_iota(jnp.int32, (16, LANES), 0)
    row32 = lax.broadcasted_iota(jnp.int32, (32, LANES), 0)

    def twice(value):
        return jnp.concatenate([value, value], axis=1)

    def choose(picks, value):
        return jnp.concatenate([jnp.where(p, value, 0.0) for p in picks], axis=1).astype(bf16)

    first16 = (row16 & 4) == 0
    first32 = (row32 & 4) == 0
    upper16 = row16 < 8
    blocks32 = [(row32 >> 3) == q for q in range(PAIRS)]

    def rows(group, size, part=0):
        start = group * (4 * GROUP) + part
        return pl.ds(start if isinstance(start, int) else pl.multiple_of(start, 16), size)

    def stacked(value, size, parts):
        return jnp.concatenate(
            [value[size * q : size * (q + 1)] for q in range(PAIRS) for _ in range(parts)], axis=0
        )

    def folded(value, size):
        return jnp.concatenate(
            [
                value[2 * size * q : 2 * size * q + size] + value[2 * size * q + size : 2 * size * (q + 1)]
                for q in range(PAIRS)
            ],
            axis=0,
        )

    def first_layer(j):
        for q in range(PAIRS):
            for a in range(2):
                s_row = jnp.broadcast_to(s_s[pl.ds(GROUP * j + 2 * q + a, 1), :], (e1, LANES))
                h1_s[j, q * e1 : (q + 1) * e1, a * LANES : (a + 1) * LANES] = jnp.tanh(
                    w1 * s_row + b1
                )

    def second_layer(j):
        h1 = h1_s[j]
        t2 = jnp.tanh(mm(w2t_ref[...], h1.astype(bf16)) + twice(b2_ref[...]))
        h2_s[j] = stacked(h1, e1, 2) + t2
        u2_s[j] = 1.0 - t2 * t2

    def third_layer(j):
        h2 = h2_s[j]
        t3 = jnp.tanh(mm(w3t_ref[...], h2.astype(bf16)) + twice(b3_ref[...]))
        g_s[j] = (stacked(h2, e2, 2) + t3).astype(bf16)
        u3_s[j] = 1.0 - t3 * t3

    def tensor(j):
        for h in range(PAIRS // 2):
            lhs = choose((first16, ~first16), r_s[rows(j, 16, 16 * h), :])
            t = mm(lhs, g_s[j, half * h : half * (h + 1), :], NT) * inv_slots
            t_s[rows(j, 16, 16 * h), :] = jnp.where(upper16, t[:, :e3], t[:, e3:])

    def pipeline(stages):
        depth = len(stages) - 1

        def run(step, valid):
            for lag in range(depth, -1, -1):
                if valid(lag):
                    stages[lag](step - lag)

        for step in range(depth):
            run(step, lambda lag: lag <= step)

        def body(step, carry):
            run(step, lambda lag: True)
            return carry

        lax.fori_loop(depth, groups, body, 0)
        for step in range(groups, groups + depth):
            run(step, lambda lag: step - lag < groups)

    pipeline([first_layer, second_layer, third_layer, tensor])

    tens = [t_s[pl.ds(c, atoms, stride=4), :] for c in range(4)]
    for k in range(m2):
        total = tens[0] * jnp.broadcast_to(tens[0][:, k : k + 1], (atoms, e3))
        for c in range(1, 4):
            total = total + tens[c] * jnp.broadcast_to(tens[c][:, k : k + 1], (atoms, e3))
        des_s[:, k * e3 : (k + 1) * e3] = total.astype(bf16)
    readout = out_ref[...]
    y1 = jnp.tanh(mm(des_s[...], f1_ref[...]) + c1_ref[...])
    t4 = jnp.tanh(mm(y1.astype(bf16), f2_ref[...]) + c2_ref[...])
    energy_ref[...] = lax.dot_general(
        readout, y1 + t4, NT, precision=lax.Precision.HIGHEST, preferred_element_type=f32
    )
    dz2 = (readout * (1.0 - t4 * t4)).astype(bf16)
    dy1 = readout + mm(dz2, f2_ref[...], NT)
    dz1 = (dy1 * (1.0 - y1 * y1)).astype(bf16)
    lane = lax.broadcasted_iota(jnp.int32, (atoms, e3), 1)
    grads = [jnp.zeros((atoms, e3), f32)] * 4
    for k in range(m2):
        dd = mm(dz1, f1_ref[k * e3 : (k + 1) * e3, :], NT)
        for c in range(4):
            other = jnp.sum(dd * tens[c], axis=1, keepdims=True)
            grads[c] = (
                grads[c]
                + dd * jnp.broadcast_to(tens[c][:, k : k + 1], (atoms, e3))
                + jnp.where(lane == k, other, 0.0)
            )
    for c in range(4):
        d_s[pl.ds(c, atoms, stride=4), :] = grads[c].astype(bf16).astype(f32) * inv_slots

    def third_back(j):
        dt = d_s[rows(j, 32), :]
        for h in range(PAIRS // 2):
            lhs = choose((upper16, ~upper16), dt[16 * h : 16 * (h + 1)])
            dr = mm(lhs, g_s[j, half * h : half * (h + 1), :])
            dr_s[rows(j, 16, 16 * h), :] = jnp.where(first16, dr[:, :LANES], dr[:, LANES:])
        spread = choose((first32, ~first32), r_s[rows(j, 32), :])
        dg = mm(choose(blocks32, dt), spread, TN)
        da3_s[j] = (dg * u3_s[j]).astype(bf16)
        dg_s[j] = folded(dg, e2)

    def second_back(j):
        back = jnp.concatenate(
            [mm(w3_ref[...], da3_s[j, half * h : half * (h + 1), :]) for h in range(PAIRS // 2)],
            axis=0,
        )
        dh2 = dg_s[j] + back
        da2_s[j] = (dh2 * u2_s[j]).astype(bf16)
        dh2_s[j] = folded(dh2, e1)

    def first_back(j):
        dh1 = dh2_s[j] + mm(w2_ref[...], da2_s[j])
        h1 = h1_s[j]
        part = dh1 * (1.0 - h1 * h1)
        for q in range(PAIRS):
            for a in range(2):
                z = None
                for i in range(0, e1, 8):
                    at = q * e1 + i
                    term = part[at : at + 8, a * LANES : (a + 1) * LANES] * w1[i : i + 8]
                    z = term if z is None else z + term
                start = (GROUP * j + 2 * q + a) * 8
                z_s[pl.ds(start if isinstance(start, int) else pl.multiple_of(start, 8), 8), :] = z

    pipeline([third_back, second_back, first_back])

    ds = dr_s[pl.ds(0, atoms, stride=4), :]
    for i in range(8):
        ds = ds + z_s[pl.ds(i, atoms, stride=8), :]
    drs = [dr_s[pl.ds(c + 1, atoms, stride=4), :] for c in range(3)]
    radial = drs[0] * disp[0] + drs[1] * disp[1] + drs[2] * disp[2]
    factor = -ds / (radius * quad) - 2.0 * radial * (inv_quad * inv_quad)
    ones = jnp.ones((8, LANES), bf16)
    zero = jnp.zeros((atoms, LANES), f32)
    sums = []
    for c in range(3):
        pull = mask * (disp[c] * factor + drs[c] * inv_quad)
        upper, lower = split2(pull)
        gr_s[pl.ds(c, atoms, stride=8), :] = upper
        gr_s[pl.ds(c + 3, atoms, stride=8), :] = lower
        both_parts = mm(ones, upper.astype(bf16), NT) + mm(ones, lower.astype(bf16), NT)
        sums.append(both_parts[0:1])
    gr_s[pl.ds(6, atoms, stride=8), :] = zero
    gr_s[pl.ds(7, atoms, stride=8), :] = zero
    mine = jnp.concatenate(sums, axis=0)

    place = lax.broadcasted_iota(jnp.int32, (LANES, LANES), 0)
    chunks = 3 * per

    def scatter(p, total):
        rows = []
        hots = []
        for i in range(2):
            atom = 2 * p + i
            values = gr_s[pl.ds(pl.multiple_of(atom * 8, 8), 8), :]
            upper = jnp.broadcast_to(high_ref[pl.ds(atom, 1), :], (8, LANES))
            lower = jnp.broadcast_to(low_ref[pl.ds(atom, 1), :], (LANES, LANES))
            rows.append(
                jnp.concatenate(
                    [jnp.where(upper == a, values, 0.0) for a in range(chunks)], axis=0
                )
            )
            hots.append(jnp.where(lower == place, 1.0, 0.0).astype(bf16))
        lhs = jnp.concatenate(rows, axis=1).astype(bf16)
        return total + mm(lhs, jnp.concatenate(hots, axis=1), NT)

    total = lax.fori_loop(0, pairs, scatter, jnp.zeros((8 * chunks, LANES), f32), unroll=4)
    rank = rank_ref[0]
    spot = lax.broadcasted_iota(jnp.int32, (3, brick_len), 1) // atoms
    placed = jnp.where(
        spot == rank, jnp.concatenate([mine] * (brick_len // atoms), axis=1), 0.0
    )
    for part, target in enumerate((to_before_ref, to_brick_ref, to_after_ref)):
        pieces = []
        for chunk in range(per):
            at = 8 * (part * per + chunk)
            pieces.append(total[at : at + 3] + total[at + 3 : at + 6])
        whole = -jnp.concatenate(pieces, axis=1)
        target[...] = whole + placed if part == 1 else whole


def column(row):
    size = row.shape[1]
    shape = (size, size)
    same = lax.broadcasted_iota(jnp.int32, shape, 0) == lax.broadcasted_iota(jnp.int32, shape, 1)
    picked = jnp.sum(jnp.where(same, jnp.broadcast_to(row, shape), 0.0), axis=1, keepdims=True)
    return jnp.broadcast_to(picked, (size, LANES))


def diagonal(target, block, copies):
    tall, long = block.shape
    target[...] = jnp.zeros(target.shape, target.dtype)
    for q in range(copies):
        target[q * tall : (q + 1) * tall, q * long : (q + 1) * long] = block


def prepare_kernel(*refs):
    count = 5
    raw = refs[:count]
    low_o, high_o, w1_o, b1_o, w2t_o, w2_o, b2_o, w3t_o, w3_o, b3_o, f1_o, c1_o, c2_o, out_o = refs[
        count : count + 14
    ]
    here = refs[count + 14 : 2 * count + 14]
    wide_s, sems = refs[2 * count + 14 :]
    copies = [pltpu.make_async_copy(raw[i], here[i], sems.at[i]) for i in range(count)]
    for copy in copies:
        copy.start()
    for copy in copies:
        copy.wait()
    nbr, w2, w3, f1, small = here
    index = nbr[...]
    low_o[...] = index & (LANES - 1)
    high_o[...] = lax.shift_right_arithmetic(index, 7)
    e1, e2 = w2.shape
    e3 = w3.shape[1]
    fit = f1.shape[0]
    rows = f1.shape[1]
    m2 = rows // e3
    vectors = []
    start = 0
    for size in (e1, e1, e2, e3, fit, fit, fit):
        vectors.append(small[:, start : start + size])
        start += size + -size % LANES
    w1, b1, b2, b3, c1, c2, out = vectors
    w1_o[...] = column(w1)
    b1_o[...] = column(b1)
    b2_o[...] = jnp.concatenate([column(b2)] * PAIRS, axis=0)
    b3_o[...] = jnp.concatenate([column(b3)] * PAIRS, axis=0)
    diagonal(w2_o, w2[...], PAIRS)
    diagonal(w3_o, w3[...], PAIRS // 2)
    diagonal(w2t_o, w2[...].astype(f32).T.astype(bf16), PAIRS)
    diagonal(w3t_o, w3[...].astype(f32).T.astype(bf16), PAIRS)
    c1_o[...] = c1
    c2_o[...] = c2
    out_o[...] = out
    for part in range(0, fit, LANES):
        upto = min(LANES, fit - part)
        for start in range(0, rows, LANES):
            block = f1[part : part + upto, start : start + LANES].astype(f32)
            if upto < LANES:
                block = jnp.concatenate([block, jnp.zeros((LANES - upto, LANES), f32)], axis=0)
            wide_s[start : start + LANES, :] = block.T
        for k in range(m2):
            picked = wide_s[pl.ds(k, e3, stride=m2), :]
            f1_o[k * e3 : (k + 1) * e3, part : part + upto] = picked[:, :upto].astype(bf16)


def prepare(neighbors, weights):
    w1, b1, w2, b2, w3, b3, f1, c1, f2, c2, out = weights
    e1, e2, e3 = w1.shape[0], w2.shape[1], w3.shape[1]
    fit = out.shape[0]
    small = jnp.concatenate(
        [jnp.pad(v, (0, -v.shape[0] % LANES)) for v in (w1, b1, b2, b3, c1, c2, out)]
    )
    raw = (neighbors, w2, w3, f1.T, small[None])
    shape = jax.ShapeDtypeStruct
    outs = (
        shape(neighbors.shape, jnp.int32),
        shape(neighbors.shape, jnp.int32),
        shape((e1, LANES), f32),
        shape((e1, LANES), f32),
        shape((PAIRS * e2, PAIRS * e1), bf16),
        shape((PAIRS * e1, PAIRS * e2), bf16),
        shape((PAIRS * e2, LANES), f32),
        shape((PAIRS * e3, PAIRS * e2), bf16),
        shape((PAIRS // 2 * e2, PAIRS // 2 * e3), bf16),
        shape((PAIRS * e3, LANES), f32),
        shape((f1.shape[0], fit), bf16),
        shape((1, fit), f32),
        shape((1, fit), f32),
        shape((1, fit), f32),
    )
    made = pl.pallas_call(
        prepare_kernel,
        out_shape=outs,
        in_specs=[pl.BlockSpec(memory_space=pltpu.HBM)] * len(raw),
        out_specs=[pl.BlockSpec(memory_space=pltpu.VMEM)] * len(outs),
        scratch_shapes=[pltpu.VMEM(x.shape, x.dtype) for x in raw]
        + [pltpu.VMEM((f1.shape[0], LANES), f32), pltpu.SemaphoreType.DMA((len(raw),))],
        compiler_params=pltpu.CompilerParams(vmem_limit_bytes=16 * 1024 * 1024),
        cost_estimate=pl.CostEstimate(flops=4_000_000, bytes_accessed=2_500_000, transcendentals=0),
        name="prepare",
    )(*raw)
    return (*made[:12], f2, *made[12:])


def evaluate(rank, before, brick, after, own, prepared):
    atoms, slots = prepared[0].shape
    brick_len = brick.shape[1]
    e1 = prepared[2].shape[0]
    e2 = prepared[4].shape[0] // PAIRS
    e3 = prepared[7].shape[0] // PAIRS
    groups = atoms // GROUP
    wide = 2 * slots
    own = jnp.concatenate([own, own], axis=1)[:, :LANES]
    vmem = pl.BlockSpec(memory_space=pltpu.VMEM)
    piece = jax.ShapeDtypeStruct((3, brick_len), f32)
    return pl.pallas_call(
        eval_kernel,
        out_shape=(jax.ShapeDtypeStruct((1, atoms), f32), piece, piece, piece),
        in_specs=[pl.BlockSpec(memory_space=pltpu.SMEM)] + [vmem] * (4 + len(prepared)),
        out_specs=[vmem] * 4,
        scratch_shapes=[
            pltpu.VMEM((atoms, slots), f32),
            pltpu.VMEM((4 * atoms, slots), f32),
            pltpu.VMEM((4 * atoms, e3), f32),
            pltpu.VMEM((4 * atoms, e3), f32),
            pltpu.VMEM((groups, PAIRS * e1, wide), f32),
            pltpu.VMEM((groups, PAIRS * e2, wide), f32),
            pltpu.VMEM((groups, PAIRS * e2, wide), f32),
            pltpu.VMEM((groups, PAIRS * e3, wide), f32),
            pltpu.VMEM((groups, PAIRS * e3, wide), bf16),
            pltpu.VMEM((groups, PAIRS * e3, wide), bf16),
            pltpu.VMEM((groups, PAIRS * e2, wide), f32),
            pltpu.VMEM((groups, PAIRS * e2, wide), bf16),
            pltpu.VMEM((groups, PAIRS * e1, wide), f32),
            pltpu.VMEM((8 * atoms, slots), f32),
            pltpu.VMEM((4 * atoms, slots), f32),
            pltpu.VMEM((8 * atoms, slots), f32),
            pltpu.VMEM((atoms, prepared[10].shape[0]), bf16),
        ],
        compiler_params=pltpu.CompilerParams(vmem_limit_bytes=40 * 1024 * 1024),
        name="evaluate",
    )(rank, before, brick, after, own, *prepared)


def ring(size, step):
    return [(i, (i + step) % size) for i in range(size)]


def flip(size, bit):
    return [(i, i ^ bit) for i in range(size)]


def few(size):
    return size <= 8 and size & (size - 1) == 0


def from_others(value, size):
    return [value] + [lax.ppermute(value, "help", flip(size, k)) for k in range(1, size)]


def gather_help(value):
    size = lax.axis_size("help")
    rank = lax.axis_index("help")
    if not few(size):
        return lax.all_gather(value, "help", axis=1, tiled=True)
    blocks = from_others(value, size)
    bit = 1
    while len(blocks) > 1:
        upper = (rank & bit) != 0
        blocks = [
            jnp.where(
                upper, jnp.concatenate([b, a], axis=1), jnp.concatenate([a, b], axis=1)
            )
            for a, b in zip(blocks[::2], blocks[1::2])
        ]
        bit *= 2
    return blocks[0]


def sum_help(value):
    size = lax.axis_size("help")
    if not few(size):
        return lax.psum(value, "help")
    blocks = from_others(value, size)
    while len(blocks) > 1:
        blocks = [a + b for a, b in zip(blocks[::2], blocks[1::2])]
    return blocks[0]


def exchange(up, down):
    size = lax.axis_size("brick")
    if size % 2:
        return lax.ppermute(up, "brick", ring(size, 1)), lax.ppermute(down, "brick", ring(size, -1))
    odd = (lax.axis_index("brick") & 1) == 1
    inner = lax.ppermute(jnp.where(odd, down, up), "brick", flip(size, 1))
    pairs = [(i, (i + 1) % size if i % 2 else (i - 1) % size) for i in range(size)]
    outer = lax.ppermute(jnp.where(odd, up, down), "brick", pairs)
    return jnp.where(odd, inner, outer), jnp.where(odd, outer, inner)


def local(positions, velocities, forces_in, neighbors, *weights):
    prepared = prepare(neighbors, weights)
    atoms = positions.shape[1]
    rank = lax.axis_index("help")
    ranks = rank.reshape(1).astype(jnp.int32)
    at = rank * atoms
    speed = velocities + kick_scale * forces_in
    coords = positions + time_step * speed
    state = gather_help(jnp.concatenate([coords, speed], axis=0))
    state, prepared = lax.optimization_barrier((state, prepared))
    brick_pos, brick_speed = state[:3], state[3:]
    own = coords
    for md_step in range(STEPS):
        before, after = exchange(brick_pos, brick_pos)
        energy, to_before, to_brick, to_after = evaluate(
            ranks, before, brick_pos, after, own, prepared
        )
        from_before, from_after = exchange(to_after, to_before)
        force = sum_help(to_brick + from_before + from_after)
        brick_speed = brick_speed + kick_scale * force
        if md_step + 1 < STEPS:
            brick_speed = brick_speed + kick_scale * force
            brick_pos = brick_pos + time_step * brick_speed
            own = lax.dynamic_slice_in_dim(brick_pos, at, atoms, axis=1)
    out = lax.dynamic_slice_in_dim(
        jnp.concatenate([brick_speed, force], axis=0), at, atoms, axis=1
    )
    return (own, out[:3], energy.reshape(atoms), out[3:])


def solution(mesh):
    spread = ("brick", "help")
    cols = P(None, spread)
    return jax.shard_map(
        local,
        mesh=mesh,
        in_specs=(cols, cols, cols, P(spread, None)) + (P(),) * 11,
        out_specs=(cols, cols, P(spread), cols),
        check_vma=False,
    )
```

```python
import functools

import jax
import jax.numpy as jnp
from jax import lax
from jax.experimental import pallas as pl
from jax.experimental.pallas import tpu as pltpu
from jax.sharding import PartitionSpec as P

STEPS = 2

kick_scale = 0.25
time_step = 0.05
LANES = 128
PAIRS = 4
GROUP = 2 * PAIRS
f32 = jnp.float32
bf16 = jnp.bfloat16
NN = (((1,), (0,)), ((), ()))
NT = (((1,), (1,)), ((), ()))
TN = (((0,), (0,)), ((), ()))


def mm(a, b, dims=NN):
    return lax.dot_general(a, b, dims, preferred_element_type=f32)


def split2(x):
    high = x.astype(bf16).astype(f32)
    return high, x - high


def column(row):
    size = row.shape[1]
    shape = (size, size)
    same = lax.broadcasted_iota(jnp.int32, shape, 0) == lax.broadcasted_iota(jnp.int32, shape, 1)
    picked = jnp.sum(jnp.where(same, jnp.broadcast_to(row, shape), 0.0), axis=1, keepdims=True)
    return jnp.broadcast_to(picked, (size, LANES))


def eval_kernel(
    rank_ref,
    before_ref,
    brick_ref,
    after_ref,
    own_ref,
    low_ref,
    high_ref,
    w1_ref,
    b1_ref,
    w2t_ref,
    w2_ref,
    b2_ref,
    w3t_ref,
    w3_ref,
    b3_ref,
    f1_ref,
    c1_ref,
    f2_ref,
    c2_ref,
    out_ref,
    energy_ref,
    to_before_ref,
    to_brick_ref,
    to_after_ref,
    b2_s,
    b3_s,
    s_s,
    r_s,
    t_s,
    d_s,
    h1_s,
    h2_s,
    u2_s,
    u3_s,
    g_s,
    da3_s,
    dg_s,
    da2_s,
    dh2_s,
    z_s,
    dr_s,
    gr_s,
    des_s,
):
    atoms, slots = low_ref.shape
    brick_len = brick_ref.shape[1]
    per = brick_len // LANES
    e1 = w1_ref.shape[1]
    e2 = b2_ref.shape[1]
    e3 = b3_ref.shape[1]
    m2 = f1_ref.shape[0] // e3
    inv_slots = 1.0 / slots
    pairs = atoms // 2

    low = low_ref[...]
    high = high_ref[...]
    mask = jnp.where(high >= 0, 1.0, 0.0).astype(f32)
    sub = lax.broadcasted_iota(jnp.int32, (atoms, slots), 0)
    coords = [jnp.zeros((atoms, slots), f32)] * 3
    for part, table in enumerate((before_ref, brick_ref, after_ref)):
        for chunk in range(per):
            hit = high == part * per + chunk
            for c in range(3):
                row = table[c : c + 1, chunk * LANES : (chunk + 1) * LANES]
                found = jnp.take_along_axis(
                    jnp.broadcast_to(row, (atoms, LANES)), low, axis=1, mode="promise_in_bounds"
                )
                coords[c] = jnp.where(hit, found, coords[c])
    shift = (
        jnp.where(high >= per, 1.0, 0.0) + jnp.where(high >= 2 * per, 1.0, 0.0) - 1.0
    ).astype(f32)
    disp = []
    for c in range(3):
        row = own_ref[c : c + 1, :]
        mine = jnp.take_along_axis(
            jnp.broadcast_to(row, (atoms, LANES)), sub, axis=1, mode="promise_in_bounds"
        )
        delta = coords[c] - mine
        if c == 0:
            delta = delta + shift
        disp.append(delta * mask)
    quad = disp[0] * disp[0] + disp[1] * disp[1] + disp[2] * disp[2] + 0.25
    radius = jnp.sqrt(quad)
    smooth = mask / radius
    inv_quad = 1.0 / quad
    s_s[...] = smooth
    r_s[pl.ds(0, atoms, stride=4), :] = smooth
    for c in range(3):
        r_s[pl.ds(c + 1, atoms, stride=4), :] = disp[c] * inv_quad

    groups = atoms // GROUP
    wide = 2 * slots
    half = 2 * e3
    w1 = column(w1_ref[...])
    b1 = column(b1_ref[...])
    b2_s[...] = jnp.concatenate([column(b2_ref[...])] * PAIRS, axis=0)
    b3_s[...] = jnp.concatenate([column(b3_ref[...])] * PAIRS, axis=0)
    row16 = lax.broadcasted_iota(jnp.int32, (16, LANES), 0)
    row32 = lax.broadcasted_iota(jnp.int32, (32, LANES), 0)

    def twice(value):
        return jnp.concatenate([value, value], axis=1)

    def choose(picks, value):
        return jnp.concatenate([jnp.where(p, value, 0.0) for p in picks], axis=1).astype(bf16)

    first16 = (row16 & 4) == 0
    first32 = (row32 & 4) == 0
    upper16 = row16 < 8
    blocks32 = [(row32 >> 3) == q for q in range(PAIRS)]

    def rows(group, size, part=0):
        start = group * (4 * GROUP) + part
        return pl.ds(start if isinstance(start, int) else pl.multiple_of(start, 16), size)

    def stacked(value, size, parts):
        return jnp.concatenate(
            [value[size * q : size * (q + 1)] for q in range(PAIRS) for _ in range(parts)], axis=0
        )

    def folded(value, size):
        return jnp.concatenate(
            [
                value[2 * size * q : 2 * size * q + size] + value[2 * size * q + size : 2 * size * (q + 1)]
                for q in range(PAIRS)
            ],
            axis=0,
        )

    def first_layer(j):
        for q in range(PAIRS):
            for a in range(2):
                s_row = jnp.broadcast_to(s_s[pl.ds(GROUP * j + 2 * q + a, 1), :], (e1, LANES))
                h1_s[j, q * e1 : (q + 1) * e1, a * LANES : (a + 1) * LANES] = jnp.tanh(
                    w1 * s_row + b1
                )

    def second_layer(j):
        h1 = h1_s[j]
        t2 = jnp.tanh(mm(w2t_ref[...], h1.astype(bf16)) + twice(b2_s[...]))
        h2_s[j] = stacked(h1, e1, 2) + t2
        u2_s[j] = 1.0 - t2 * t2

    def third_layer(j):
        h2 = h2_s[j]
        t3 = jnp.tanh(mm(w3t_ref[...], h2.astype(bf16)) + twice(b3_s[...]))
        g_s[j] = (stacked(h2, e2, 2) + t3).astype(bf16)
        u3_s[j] = 1.0 - t3 * t3

    def tensor(j):
        for h in range(PAIRS // 2):
            lhs = choose((first16, ~first16), r_s[rows(j, 16, 16 * h), :])
            t = mm(lhs, g_s[j, half * h : half * (h + 1), :], NT) * inv_slots
            t_s[rows(j, 16, 16 * h), :] = jnp.where(upper16, t[:, :e3], t[:, e3:])

    def pipeline(stages):
        depth = len(stages) - 1

        def run(step, valid):
            for lag in range(depth, -1, -1):
                if valid(lag):
                    stages[lag](step - lag)

        for step in range(depth):
            run(step, lambda lag: lag <= step)

        def body(step, carry):
            run(step, lambda lag: True)
            return carry

        lax.fori_loop(depth, groups, body, 0)
        for step in range(groups, groups + depth):
            run(step, lambda lag: step - lag < groups)

    pipeline([first_layer, second_layer, third_layer, tensor])

    tens = [t_s[pl.ds(c, atoms, stride=4), :] for c in range(4)]
    for k in range(m2):
        total = tens[0] * jnp.broadcast_to(tens[0][:, k : k + 1], (atoms, e3))
        for c in range(1, 4):
            total = total + tens[c] * jnp.broadcast_to(tens[c][:, k : k + 1], (atoms, e3))
        des_s[:, k * e3 : (k + 1) * e3] = total.astype(bf16)
    readout = out_ref[...]
    y1 = jnp.tanh(mm(des_s[...], f1_ref[...]) + c1_ref[...])
    t4 = jnp.tanh(mm(y1.astype(bf16), f2_ref[...]) + c2_ref[...])
    energy_ref[...] = lax.dot_general(
        readout, y1 + t4, NT, precision=lax.Precision.HIGHEST, preferred_element_type=f32
    )
    dz2 = (readout * (1.0 - t4 * t4)).astype(bf16)
    dy1 = readout + mm(dz2, f2_ref[...], NT)
    dz1 = (dy1 * (1.0 - y1 * y1)).astype(bf16)
    lane = lax.broadcasted_iota(jnp.int32, (atoms, e3), 1)
    grads = [jnp.zeros((atoms, e3), f32)] * 4
    for k in range(m2):
        dd = mm(dz1, f1_ref[k * e3 : (k + 1) * e3, :], NT)
        for c in range(4):
            other = jnp.sum(dd * tens[c], axis=1, keepdims=True)
            grads[c] = (
                grads[c]
                + dd * jnp.broadcast_to(tens[c][:, k : k + 1], (atoms, e3))
                + jnp.where(lane == k, other, 0.0)
            )
    for c in range(4):
        d_s[pl.ds(c, atoms, stride=4), :] = grads[c].astype(bf16).astype(f32) * inv_slots

    def third_back(j):
        dt = d_s[rows(j, 32), :]
        for h in range(PAIRS // 2):
            lhs = choose((upper16, ~upper16), dt[16 * h : 16 * (h + 1)])
            dr = mm(lhs, g_s[j, half * h : half * (h + 1), :])
            dr_s[rows(j, 16, 16 * h), :] = jnp.where(first16, dr[:, :LANES], dr[:, LANES:])
        spread = choose((first32, ~first32), r_s[rows(j, 32), :])
        dg = mm(choose(blocks32, dt), spread, TN)
        da3_s[j] = (dg * u3_s[j]).astype(bf16)
        dg_s[j] = folded(dg, e2)

    def second_back(j):
        back = jnp.concatenate(
            [mm(w3_ref[...], da3_s[j, half * h : half * (h + 1), :]) for h in range(PAIRS // 2)],
            axis=0,
        )
        dh2 = dg_s[j] + back
        da2_s[j] = (dh2 * u2_s[j]).astype(bf16)
        dh2_s[j] = folded(dh2, e1)

    def first_back(j):
        dh1 = dh2_s[j] + mm(w2_ref[...], da2_s[j])
        h1 = h1_s[j]
        part = dh1 * (1.0 - h1 * h1)
        for q in range(PAIRS):
            for a in range(2):
                z = None
                for i in range(0, e1, 8):
                    at = q * e1 + i
                    term = part[at : at + 8, a * LANES : (a + 1) * LANES] * w1[i : i + 8]
                    z = term if z is None else z + term
                start = (GROUP * j + 2 * q + a) * 8
                z_s[pl.ds(start if isinstance(start, int) else pl.multiple_of(start, 8), 8), :] = z

    pipeline([third_back, second_back, first_back])

    ds = dr_s[pl.ds(0, atoms, stride=4), :]
    for i in range(8):
        ds = ds + z_s[pl.ds(i, atoms, stride=8), :]
    drs = [dr_s[pl.ds(c + 1, atoms, stride=4), :] for c in range(3)]
    radial = drs[0] * disp[0] + drs[1] * disp[1] + drs[2] * disp[2]
    factor = -ds / (radius * quad) - 2.0 * radial * (inv_quad * inv_quad)
    ones = jnp.ones((8, LANES), bf16)
    zero = jnp.zeros((atoms, LANES), f32)
    sums = []
    for c in range(3):
        pull = mask * (disp[c] * factor + drs[c] * inv_quad)
        upper, lower = split2(pull)
        gr_s[pl.ds(c, atoms, stride=8), :] = upper
        gr_s[pl.ds(c + 3, atoms, stride=8), :] = lower
        both_parts = mm(ones, upper.astype(bf16), NT) + mm(ones, lower.astype(bf16), NT)
        sums.append(both_parts[0:1])
    gr_s[pl.ds(6, atoms, stride=8), :] = zero
    gr_s[pl.ds(7, atoms, stride=8), :] = zero
    mine = jnp.concatenate(sums, axis=0)

    place = lax.broadcasted_iota(jnp.int32, (LANES, LANES), 0)
    chunks = 3 * per

    def scatter(p, total):
        rows = []
        hots = []
        for i in range(2):
            atom = 2 * p + i
            values = gr_s[pl.ds(pl.multiple_of(atom * 8, 8), 8), :]
            upper = jnp.broadcast_to(high_ref[pl.ds(atom, 1), :], (8, LANES))
            lower = jnp.broadcast_to(low_ref[pl.ds(atom, 1), :], (LANES, LANES))
            rows.append(
                jnp.concatenate(
                    [jnp.where(upper == a, values, 0.0) for a in range(chunks)], axis=0
                )
            )
            hots.append(jnp.where(lower == place, 1.0, 0.0).astype(bf16))
        lhs = jnp.concatenate(rows, axis=1).astype(bf16)
        return total + mm(lhs, jnp.concatenate(hots, axis=1), NT)

    total = lax.fori_loop(0, pairs, scatter, jnp.zeros((8 * chunks, LANES), f32), unroll=4)
    rank = rank_ref[0]
    spot = lax.broadcasted_iota(jnp.int32, (3, brick_len), 1) // atoms
    placed = jnp.where(
        spot == rank, jnp.concatenate([mine] * (brick_len // atoms), axis=1), 0.0
    )
    for part, target in enumerate((to_before_ref, to_brick_ref, to_after_ref)):
        pieces = []
        for chunk in range(per):
            at = 8 * (part * per + chunk)
            pieces.append(total[at : at + 3] + total[at + 3 : at + 6])
        whole = -jnp.concatenate(pieces, axis=1)
        target[...] = whole + placed if part == 1 else whole


def diagonal(target, block, copies):
    tall, long = block.shape
    target[...] = jnp.zeros(target.shape, target.dtype)
    for q in range(copies):
        target[q * tall : (q + 1) * tall, q * long : (q + 1) * long] = block


def prepare_kernel(*refs):
    count = 4
    raw = refs[:count]
    low_o, high_o, w2t_o, w2_o, w3t_o, w3_o, f1_o = refs[count : count + 7]
    here = refs[count + 7 : 2 * count + 7]
    wide_s, sems = refs[2 * count + 7 :]
    copies = [pltpu.make_async_copy(raw[i], here[i], sems.at[i]) for i in range(count)]
    for copy in copies:
        copy.start()
    for copy in copies:
        copy.wait()
    nbr, w2, w3, f1 = here
    index = nbr[...]
    low_o[...] = index & (LANES - 1)
    high_o[...] = lax.shift_right_arithmetic(index, 7)
    e3 = w3.shape[1]
    fit, rows = f1.shape
    m2 = rows // e3
    diagonal(w2_o, w2[...], PAIRS)
    diagonal(w3_o, w3[...], PAIRS // 2)
    diagonal(w2t_o, w2[...].astype(f32).T.astype(bf16), PAIRS)
    diagonal(w3t_o, w3[...].astype(f32).T.astype(bf16), PAIRS)
    for part in range(0, fit, LANES):
        upto = min(LANES, fit - part)
        for start in range(0, rows, LANES):
            block = f1[part : part + upto, start : start + LANES].astype(f32)
            if upto < LANES:
                block = jnp.concatenate([block, jnp.zeros((LANES - upto, LANES), f32)], axis=0)
            wide_s[start : start + LANES, :] = block.T
        for k in range(m2):
            picked = wide_s[pl.ds(k, e3, stride=m2), :]
            f1_o[k * e3 : (k + 1) * e3, part : part + upto] = picked[:, :upto].astype(bf16)


def prepare(neighbors, weights):
    w1, b1, w2, b2, w3, b3, f1, c1, f2, c2, out = weights
    e1, e2, e3 = w1.shape[0], w2.shape[1], w3.shape[1]
    fit = out.shape[0]
    raw = (neighbors, w2, w3, f1.T)
    shape = jax.ShapeDtypeStruct
    outs = (
        shape(neighbors.shape, jnp.int32),
        shape(neighbors.shape, jnp.int32),
        shape((PAIRS * e2, PAIRS * e1), bf16),
        shape((PAIRS * e1, PAIRS * e2), bf16),
        shape((PAIRS * e3, PAIRS * e2), bf16),
        shape((PAIRS // 2 * e2, PAIRS // 2 * e3), bf16),
        shape((f1.shape[0], fit), bf16),
    )
    made = pl.pallas_call(
        prepare_kernel,
        out_shape=outs,
        in_specs=[pl.BlockSpec(memory_space=pltpu.HBM)] * len(raw),
        out_specs=[pl.BlockSpec(memory_space=pltpu.VMEM)] * len(outs),
        scratch_shapes=[pltpu.VMEM(x.shape, x.dtype) for x in raw]
        + [pltpu.VMEM((f1.shape[0], LANES), f32), pltpu.SemaphoreType.DMA((len(raw),))],
        compiler_params=pltpu.CompilerParams(vmem_limit_bytes=16 * 1024 * 1024),
        cost_estimate=pl.CostEstimate(flops=4_000_000, bytes_accessed=2_500_000, transcendentals=0),
        name="prepare",
    )(*raw)
    low, high, w2t, w2, w3t, w3, f1 = made
    return (
        low,
        high,
        w1[None],
        b1[None],
        w2t,
        w2,
        b2[None],
        w3t,
        w3,
        b3[None],
        f1,
        c1[None],
        f2,
        c2[None],
        out[None],
    )


def evaluate(rank, before, brick, after, own, prepared):
    atoms, slots = prepared[0].shape
    brick_len = brick.shape[1]
    e1, e2, e3 = (prepared[i].shape[1] for i in (2, 6, 9))
    groups = atoms // GROUP
    wide = 2 * slots
    own = jnp.concatenate([own, own], axis=1)[:, :LANES]
    vmem = pl.BlockSpec(memory_space=pltpu.VMEM)
    piece = jax.ShapeDtypeStruct((3, brick_len), f32)
    return pl.pallas_call(
        eval_kernel,
        out_shape=(jax.ShapeDtypeStruct((1, atoms), f32), piece, piece, piece),
        in_specs=[pl.BlockSpec(memory_space=pltpu.SMEM)] + [vmem] * (4 + len(prepared)),
        out_specs=[vmem] * 4,
        scratch_shapes=[
            pltpu.VMEM((PAIRS * e2, LANES), f32),
            pltpu.VMEM((PAIRS * e3, LANES), f32),
            pltpu.VMEM((atoms, slots), f32),
            pltpu.VMEM((4 * atoms, slots), f32),
            pltpu.VMEM((4 * atoms, e3), f32),
            pltpu.VMEM((4 * atoms, e3), f32),
            pltpu.VMEM((groups, PAIRS * e1, wide), f32),
            pltpu.VMEM((groups, PAIRS * e2, wide), f32),
            pltpu.VMEM((groups, PAIRS * e2, wide), f32),
            pltpu.VMEM((groups, PAIRS * e3, wide), f32),
            pltpu.VMEM((groups, PAIRS * e3, wide), bf16),
            pltpu.VMEM((groups, PAIRS * e3, wide), bf16),
            pltpu.VMEM((groups, PAIRS * e2, wide), f32),
            pltpu.VMEM((groups, PAIRS * e2, wide), bf16),
            pltpu.VMEM((groups, PAIRS * e1, wide), f32),
            pltpu.VMEM((8 * atoms, slots), f32),
            pltpu.VMEM((4 * atoms, slots), f32),
            pltpu.VMEM((8 * atoms, slots), f32),
            pltpu.VMEM((atoms, prepared[10].shape[0]), bf16),
        ],
        compiler_params=pltpu.CompilerParams(vmem_limit_bytes=40 * 1024 * 1024),
        name="evaluate",
    )(rank, before, brick, after, own, *prepared)


def ring(size, step):
    return [(i, (i + step) % size) for i in range(size)]


def flip(size, bit):
    return [(i, i ^ bit) for i in range(size)]


def few(size):
    return size <= 8 and size & (size - 1) == 0


def from_others(value, size):
    return [value] + [lax.ppermute(value, "help", flip(size, k)) for k in range(1, size)]


def gather_help(value):
    size = lax.axis_size("help")
    rank = lax.axis_index("help")
    if not few(size):
        return lax.all_gather(value, "help", axis=1, tiled=True)
    blocks = from_others(value, size)
    bit = 1
    while len(blocks) > 1:
        upper = (rank & bit) != 0
        blocks = [
            jnp.where(
                upper, jnp.concatenate([b, a], axis=1), jnp.concatenate([a, b], axis=1)
            )
            for a, b in zip(blocks[::2], blocks[1::2])
        ]
        bit *= 2
    return blocks[0]


def sum_help(value):
    size = lax.axis_size("help")
    if not few(size):
        return lax.psum(value, "help")
    blocks = from_others(value, size)
    while len(blocks) > 1:
        blocks = [a + b for a, b in zip(blocks[::2], blocks[1::2])]
    return blocks[0]


def exchange(up, down):
    size = lax.axis_size("brick")
    if size % 2:
        return lax.ppermute(up, "brick", ring(size, 1)), lax.ppermute(down, "brick", ring(size, -1))
    odd = (lax.axis_index("brick") & 1) == 1
    inner = lax.ppermute(jnp.where(odd, down, up), "brick", flip(size, 1))
    pairs = [(i, (i + 1) % size if i % 2 else (i - 1) % size) for i in range(size)]
    outer = lax.ppermute(jnp.where(odd, up, down), "brick", pairs)
    return jnp.where(odd, inner, outer), jnp.where(odd, outer, inner)


def local(positions, velocities, forces_in, neighbors, *weights):
    prepared = prepare(neighbors, weights)
    atoms = positions.shape[1]
    rank = lax.axis_index("help")
    ranks = rank.reshape(1).astype(jnp.int32)
    at = rank * atoms
    speed = velocities + kick_scale * forces_in
    coords = positions + time_step * speed
    state = gather_help(jnp.concatenate([coords, speed], axis=0))
    state, made = lax.optimization_barrier((state, prepared[:2]))
    prepared = (*made, *prepared[2:])
    brick_pos, brick_speed = state[:3], state[3:]
    own = coords
    for md_step in range(STEPS):
        before, after = exchange(brick_pos, brick_pos)
        energy, to_before, to_brick, to_after = evaluate(
            ranks, before, brick_pos, after, own, prepared
        )
        from_before, from_after = exchange(to_after, to_before)
        force = sum_help(to_brick + from_before + from_after)
        brick_speed = brick_speed + kick_scale * force
        if md_step + 1 < STEPS:
            brick_speed = brick_speed + kick_scale * force
            brick_pos = brick_pos + time_step * brick_speed
            own = lax.dynamic_slice_in_dim(brick_pos, at, atoms, axis=1)
    out = lax.dynamic_slice_in_dim(
        jnp.concatenate([brick_speed, force], axis=0), at, atoms, axis=1
    )
    return (own, out[:3], energy.reshape(atoms), out[3:])


def solution(mesh):
    spread = ("brick", "help")
    cols = P(None, spread)
    return jax.shard_map(
        local,
        mesh=mesh,
        in_specs=(cols, cols, cols, P(spread, None)) + (P(),) * 11,
        out_specs=(cols, cols, P(spread), cols),
        check_vma=False,
    )
```

```python
import functools

import jax
import jax.numpy as jnp
from jax import lax
from jax.experimental import pallas as pl
from jax.experimental.pallas import tpu as pltpu
from jax.sharding import PartitionSpec as P

STEPS = 2

kick_scale = 0.25
time_step = 0.05
LANES = 128
PAIRS = 4
GROUP = 2 * PAIRS
f32 = jnp.float32
bf16 = jnp.bfloat16
NN = (((1,), (0,)), ((), ()))
NT = (((1,), (1,)), ((), ()))
TN = (((0,), (0,)), ((), ()))


def mm(a, b, dims=NN):
    return lax.dot_general(a, b, dims, preferred_element_type=f32)


def split2(x):
    high = x.astype(bf16).astype(f32)
    return high, x - high


def column(row):
    size = row.shape[1]
    shape = (size, size)
    same = lax.broadcasted_iota(jnp.int32, shape, 0) == lax.broadcasted_iota(jnp.int32, shape, 1)
    picked = jnp.sum(jnp.where(same, jnp.broadcast_to(row, shape), 0.0), axis=1, keepdims=True)
    return jnp.broadcast_to(picked, (size, LANES))


def eval_kernel(
    rank_ref,
    before_ref,
    brick_ref,
    after_ref,
    own_ref,
    low_ref,
    high_ref,
    w1_ref,
    b1_ref,
    w2t_ref,
    w2_ref,
    b2_ref,
    w3t_ref,
    w3_ref,
    b3_ref,
    f1_ref,
    c1_ref,
    f2_ref,
    c2_ref,
    out_ref,
    energy_ref,
    to_before_ref,
    to_brick_ref,
    to_after_ref,
    b2_s,
    b3_s,
    s_s,
    r_s,
    t_s,
    d_s,
    h1_s,
    h2_s,
    u2_s,
    u3_s,
    g_s,
    da3_s,
    dg_s,
    da2_s,
    dh2_s,
    z_s,
    dr_s,
    gr_s,
    des_s,
    bc_s,
    dd_s,
    pull_s,
):
    atoms, slots = low_ref.shape
    brick_len = brick_ref.shape[1]
    per = brick_len // LANES
    e1 = w1_ref.shape[1]
    e2 = b2_ref.shape[1]
    e3 = b3_ref.shape[1]
    m2 = f1_ref.shape[0] // e3
    inv_slots = 1.0 / slots

    low = low_ref[...]
    high = high_ref[...]
    mask = jnp.where(high >= 0, 1.0, 0.0).astype(f32)
    sub = lax.broadcasted_iota(jnp.int32, (atoms, slots), 0)
    coords = [jnp.zeros((atoms, slots), f32)] * 3
    for part, table in enumerate((before_ref, brick_ref, after_ref)):
        for chunk in range(per):
            hit = high == part * per + chunk
            for c in range(3):
                row = table[c : c + 1, chunk * LANES : (chunk + 1) * LANES]
                found = jnp.take_along_axis(
                    jnp.broadcast_to(row, (atoms, LANES)), low, axis=1, mode="promise_in_bounds"
                )
                coords[c] = jnp.where(hit, found, coords[c])
    shift = (
        jnp.where(high >= per, 1.0, 0.0) + jnp.where(high >= 2 * per, 1.0, 0.0) - 1.0
    ).astype(f32)
    disp = []
    for c in range(3):
        row = own_ref[c : c + 1, :]
        mine = jnp.take_along_axis(
            jnp.broadcast_to(row, (atoms, LANES)), sub, axis=1, mode="promise_in_bounds"
        )
        delta = coords[c] - mine
        if c == 0:
            delta = delta + shift
        disp.append(delta * mask)
    quad = disp[0] * disp[0] + disp[1] * disp[1] + disp[2] * disp[2] + 0.25
    radius = jnp.sqrt(quad)
    smooth = mask / radius
    inv_quad = 1.0 / quad
    s_s[...] = smooth
    r_s[pl.ds(0, atoms, stride=4), :] = smooth
    for c in range(3):
        r_s[pl.ds(c + 1, atoms, stride=4), :] = disp[c] * inv_quad

    groups = atoms // GROUP
    wide = 2 * slots
    half = 2 * e3
    w1 = column(w1_ref[...])
    b1 = column(b1_ref[...])
    b2_s[...] = jnp.concatenate([column(b2_ref[...])] * PAIRS, axis=0)
    b3_s[...] = jnp.concatenate([column(b3_ref[...])] * PAIRS, axis=0)
    row16 = lax.broadcasted_iota(jnp.int32, (16, LANES), 0)
    row32 = lax.broadcasted_iota(jnp.int32, (32, LANES), 0)

    def twice(value):
        return jnp.concatenate([value, value], axis=1)

    def choose(picks, value):
        return jnp.concatenate([jnp.where(p, value, 0.0) for p in picks], axis=1).astype(bf16)

    first16 = (row16 & 4) == 0
    first32 = (row32 & 4) == 0
    upper16 = row16 < 8
    blocks32 = [(row32 >> 3) == q for q in range(PAIRS)]

    def rows(group, size, part=0):
        start = group * (4 * GROUP) + part
        return pl.ds(start if isinstance(start, int) else pl.multiple_of(start, 16), size)

    def stacked(value, size, parts):
        return jnp.concatenate(
            [value[size * q : size * (q + 1)] for q in range(PAIRS) for _ in range(parts)], axis=0
        )

    def folded(value, size):
        return jnp.concatenate(
            [
                value[2 * size * q : 2 * size * q + size] + value[2 * size * q + size : 2 * size * (q + 1)]
                for q in range(PAIRS)
            ],
            axis=0,
        )

    def first_layer(j):
        for q in range(PAIRS):
            for a in range(2):
                s_row = jnp.broadcast_to(s_s[pl.ds(GROUP * j + 2 * q + a, 1), :], (e1, LANES))
                h1_s[j, q * e1 : (q + 1) * e1, a * LANES : (a + 1) * LANES] = jnp.tanh(
                    w1 * s_row + b1
                )

    def second_layer(j):
        h1 = h1_s[j]
        t2 = jnp.tanh(mm(w2t_ref[...], h1.astype(bf16)) + twice(b2_s[...]))
        h2_s[j] = stacked(h1, e1, 2) + t2
        u2_s[j] = 1.0 - t2 * t2

    def third_layer(j):
        h2 = h2_s[j]
        t3 = jnp.tanh(mm(w3t_ref[...], h2.astype(bf16)) + twice(b3_s[...]))
        g_s[j] = (stacked(h2, e2, 2) + t3).astype(bf16)
        u3_s[j] = 1.0 - t3 * t3

    def tensor(j):
        for h in range(PAIRS // 2):
            lhs = choose((first16, ~first16), r_s[rows(j, 16, 16 * h), :])
            t = mm(lhs, g_s[j, half * h : half * (h + 1), :], NT) * inv_slots
            t_s[rows(j, 16, 16 * h), :] = jnp.where(upper16, t[:, :e3], t[:, e3:])

    def descriptor(j):
        at = slice(GROUP * j, GROUP * (j + 1))
        t = [t_s[pl.ds(4 * GROUP * j + c, GROUP, stride=4), :] for c in range(4)]
        pair = []
        for k in range(m2):
            total = None
            for c in range(4):
                factor = jnp.broadcast_to(t[c][:, k : k + 1], (GROUP, e3))
                bc_s[c * m2 + k, at, :] = factor
                total = t[c] * factor if total is None else total + t[c] * factor
            pair.append(total)
            if len(pair) == 2:
                des_s[at, (k - 1) * e3 : (k + 1) * e3] = jnp.concatenate(pair, axis=1).astype(bf16)
                pair = []

    def pipeline(stages):
        depth = len(stages) - 1

        def run(step, valid):
            for lag in range(depth, -1, -1):
                if valid(lag):
                    stages[lag](step - lag)

        for step in range(groups + depth):
            run(step, lambda lag: 0 <= step - lag < groups)

    pipeline([first_layer, second_layer, third_layer, tensor, descriptor])

    readout = out_ref[...]
    y1 = jnp.tanh(mm(des_s[...], f1_ref[...]) + c1_ref[...])
    t4 = jnp.tanh(mm(y1.astype(bf16), f2_ref[...]) + c2_ref[...])
    energy_ref[...] = lax.dot_general(
        readout, y1 + t4, NT, precision=lax.Precision.HIGHEST, preferred_element_type=f32
    )
    dz2 = (readout * (1.0 - t4 * t4)).astype(bf16)
    dy1 = readout + mm(dz2, f2_ref[...], NT)
    dz1 = (dy1 * (1.0 - y1 * y1)).astype(bf16)
    dd_s[...] = mm(dz1, f1_ref[...], NT)
    lane = lax.broadcasted_iota(jnp.int32, (GROUP, e3), 1)

    def tensor_back(j):
        at = slice(GROUP * j, GROUP * (j + 1))
        t = [t_s[pl.ds(4 * GROUP * j + c, GROUP, stride=4), :] for c in range(4)]
        grads = [None] * 4
        others = [jnp.zeros((GROUP, e3), f32)] * 4
        for k in range(m2):
            dd = dd_s[at, k * e3 : (k + 1) * e3]
            for c in range(4):
                other = jnp.sum(dd * t[c], axis=1, keepdims=True)
                others[c] = jnp.where(lane == k, other, others[c])
                term = dd * bc_s[c * m2 + k, at, :]
                grads[c] = term if grads[c] is None else grads[c] + term
        for c in range(4):
            rounded = (grads[c] + others[c]).astype(bf16).astype(f32)
            d_s[pl.ds(4 * GROUP * j + c, GROUP, stride=4), :] = rounded * inv_slots

    def third_back(j):
        dt = d_s[rows(j, 32), :]
        for h in range(PAIRS // 2):
            lhs = choose((upper16, ~upper16), dt[16 * h : 16 * (h + 1)])
            dr = mm(lhs, g_s[j, half * h : half * (h + 1), :])
            dr_s[rows(j, 16, 16 * h), :] = jnp.where(first16, dr[:, :LANES], dr[:, LANES:])
        spread = choose((first32, ~first32), r_s[rows(j, 32), :])
        dg = mm(choose(blocks32, dt), spread, TN)
        da3_s[j] = (dg * u3_s[j]).astype(bf16)
        dg_s[j] = folded(dg, e2)

    def second_back(j):
        back = jnp.concatenate(
            [mm(w3_ref[...], da3_s[j, half * h : half * (h + 1), :]) for h in range(PAIRS // 2)],
            axis=0,
        )
        dh2 = dg_s[j] + back
        da2_s[j] = (dh2 * u2_s[j]).astype(bf16)
        dh2_s[j] = folded(dh2, e1)

    def first_back(j):
        dh1 = dh2_s[j] + mm(w2_ref[...], da2_s[j])
        h1 = h1_s[j]
        part = dh1 * (1.0 - h1 * h1)
        for q in range(PAIRS):
            for a in range(2):
                z = None
                for i in range(0, e1, 8):
                    at = q * e1 + i
                    term = part[at : at + 8, a * LANES : (a + 1) * LANES] * w1[i : i + 8]
                    z = term if z is None else z + term
                start = (GROUP * j + 2 * q + a) * 8
                z_s[pl.ds(start if isinstance(start, int) else pl.multiple_of(start, 8), 8), :] = z

    ones = jnp.ones((8, LANES), bf16)
    place = lax.broadcasted_iota(jnp.int32, (LANES, LANES), 0)
    chunks = 3 * per
    mine = []
    found = [jnp.zeros((8 * chunks, LANES), f32)]

    def pulls(j):
        at = slice(GROUP * j, GROUP * (j + 1))
        drs = [dr_s[pl.ds(4 * GROUP * j + c, GROUP, stride=4), :] for c in range(4)]
        ds = drs[0]
        for i in range(8):
            ds = ds + z_s[pl.ds(8 * GROUP * j + i, GROUP, stride=8), :]
        d = [disp[c][at] for c in range(3)]
        q, iq = quad[at], inv_quad[at]
        radial = drs[1] * d[0] + drs[2] * d[1] + drs[3] * d[2]
        factor = -ds / (radius[at] * q) - 2.0 * radial * (iq * iq)
        for c in range(3):
            pull = mask[at] * (d[c] * factor + drs[c + 1] * iq)
            upper, lower = split2(pull)
            gr_s[pl.ds(8 * GROUP * j + c, GROUP, stride=8), :] = upper
            gr_s[pl.ds(8 * GROUP * j + c + 3, GROUP, stride=8), :] = lower
            pull_s[c, at, :] = upper
            pull_s[c + 3, at, :] = lower
        for c in (6, 7):
            gr_s[pl.ds(8 * GROUP * j + c, GROUP, stride=8), :] = jnp.zeros((GROUP, LANES), f32)

    def scatter(j):
        for q in range(PAIRS):
            rows_of = []
            hots = []
            for a in range(2):
                atom = GROUP * j + 2 * q + a
                values = gr_s[8 * atom : 8 * atom + 8, :]
                upper = jnp.broadcast_to(high_ref[atom : atom + 1, :], (8, LANES))
                lower = jnp.broadcast_to(low_ref[atom : atom + 1, :], (LANES, LANES))
                rows_of.append(
                    jnp.concatenate(
                        [jnp.where(upper == i, values, 0.0) for i in range(chunks)], axis=0
                    )
                )
                hots.append(jnp.where(lower == place, 1.0, 0.0).astype(bf16))
            lhs = jnp.concatenate(rows_of, axis=1).astype(bf16)
            found[0] = found[0] + mm(lhs, jnp.concatenate(hots, axis=1), NT)

    pipeline([tensor_back, third_back, second_back, first_back, pulls, scatter])
    for c in range(3):
        sums = mm(ones, pull_s[c].astype(bf16), NT) + mm(ones, pull_s[c + 3].astype(bf16), NT)
        mine.append(sums[0:1])
    mine = jnp.concatenate(mine, axis=0)
    total = found[0]
    rank = rank_ref[0]
    spot = lax.broadcasted_iota(jnp.int32, (3, brick_len), 1) // atoms
    placed = jnp.where(
        spot == rank, jnp.concatenate([mine] * (brick_len // atoms), axis=1), 0.0
    )
    for part, target in enumerate((to_before_ref, to_brick_ref, to_after_ref)):
        pieces = []
        for chunk in range(per):
            at = 8 * (part * per + chunk)
            pieces.append(total[at : at + 3] + total[at + 3 : at + 6])
        whole = -jnp.concatenate(pieces, axis=1)
        target[...] = whole + placed if part == 1 else whole


def diagonal(target, block, copies):
    tall, long = block.shape
    target[...] = jnp.zeros(target.shape, target.dtype)
    for q in range(copies):
        target[q * tall : (q + 1) * tall, q * long : (q + 1) * long] = block


def prepare_kernel(*refs):
    count = 4
    raw = refs[:count]
    low_o, high_o, w2t_o, w2_o, w3t_o, w3_o, f1_o = refs[count : count + 7]
    here = refs[count + 7 : 2 * count + 7]
    wide_s, sems = refs[2 * count + 7 :]
    copies = [pltpu.make_async_copy(raw[i], here[i], sems.at[i]) for i in range(count)]
    for copy in copies:
        copy.start()
    for copy in copies:
        copy.wait()
    nbr, w2, w3, f1 = here
    index = nbr[...]
    low_o[...] = index & (LANES - 1)
    high_o[...] = lax.shift_right_arithmetic(index, 7)
    e3 = w3.shape[1]
    fit, rows = f1.shape
    m2 = rows // e3
    diagonal(w2_o, w2[...], PAIRS)
    diagonal(w3_o, w3[...], PAIRS // 2)
    diagonal(w2t_o, w2[...].astype(f32).T.astype(bf16), PAIRS)
    diagonal(w3t_o, w3[...].astype(f32).T.astype(bf16), PAIRS)
    for part in range(0, fit, LANES):
        upto = min(LANES, fit - part)
        for start in range(0, rows, LANES):
            block = f1[part : part + upto, start : start + LANES].astype(f32)
            if upto < LANES:
                block = jnp.concatenate([block, jnp.zeros((LANES - upto, LANES), f32)], axis=0)
            wide_s[start : start + LANES, :] = block.T
        for k in range(m2):
            picked = wide_s[pl.ds(k, e3, stride=m2), :]
            f1_o[k * e3 : (k + 1) * e3, part : part + upto] = picked[:, :upto].astype(bf16)


def prepare(neighbors, weights):
    w1, b1, w2, b2, w3, b3, f1, c1, f2, c2, out = weights
    e1, e2, e3 = w1.shape[0], w2.shape[1], w3.shape[1]
    fit = out.shape[0]
    raw = (neighbors, w2, w3, f1.T)
    shape = jax.ShapeDtypeStruct
    outs = (
        shape(neighbors.shape, jnp.int32),
        shape(neighbors.shape, jnp.int32),
        shape((PAIRS * e2, PAIRS * e1), bf16),
        shape((PAIRS * e1, PAIRS * e2), bf16),
        shape((PAIRS * e3, PAIRS * e2), bf16),
        shape((PAIRS // 2 * e2, PAIRS // 2 * e3), bf16),
        shape((f1.shape[0], fit), bf16),
    )
    made = pl.pallas_call(
        prepare_kernel,
        out_shape=outs,
        in_specs=[pl.BlockSpec(memory_space=pltpu.HBM)] * len(raw),
        out_specs=[pl.BlockSpec(memory_space=pltpu.VMEM)] * len(outs),
        scratch_shapes=[pltpu.VMEM(x.shape, x.dtype) for x in raw]
        + [pltpu.VMEM((f1.shape[0], LANES), f32), pltpu.SemaphoreType.DMA((len(raw),))],
        compiler_params=pltpu.CompilerParams(vmem_limit_bytes=16 * 1024 * 1024),
        cost_estimate=pl.CostEstimate(flops=4_000_000, bytes_accessed=2_500_000, transcendentals=0),
        name="prepare",
    )(*raw)
    low, high, w2t, w2, w3t, w3, f1 = made
    return (
        low,
        high,
        w1[None],
        b1[None],
        w2t,
        w2,
        b2[None],
        w3t,
        w3,
        b3[None],
        f1,
        c1[None],
        f2,
        c2[None],
        out[None],
    )


def evaluate(rank, before, brick, after, own, prepared):
    atoms, slots = prepared[0].shape
    brick_len = brick.shape[1]
    e1, e2, e3 = (prepared[i].shape[1] for i in (2, 6, 9))
    groups = atoms // GROUP
    wide = 2 * slots
    own = jnp.concatenate([own, own], axis=1)[:, :LANES]
    vmem = pl.BlockSpec(memory_space=pltpu.VMEM)
    piece = jax.ShapeDtypeStruct((3, brick_len), f32)
    return pl.pallas_call(
        eval_kernel,
        out_shape=(jax.ShapeDtypeStruct((1, atoms), f32), piece, piece, piece),
        in_specs=[pl.BlockSpec(memory_space=pltpu.SMEM)] + [vmem] * (4 + len(prepared)),
        out_specs=[vmem] * 4,
        scratch_shapes=[
            pltpu.VMEM((PAIRS * e2, LANES), f32),
            pltpu.VMEM((PAIRS * e3, LANES), f32),
            pltpu.VMEM((atoms, slots), f32),
            pltpu.VMEM((4 * atoms, slots), f32),
            pltpu.VMEM((4 * atoms, e3), f32),
            pltpu.VMEM((4 * atoms, e3), f32),
            pltpu.VMEM((groups, PAIRS * e1, wide), f32),
            pltpu.VMEM((groups, PAIRS * e2, wide), f32),
            pltpu.VMEM((groups, PAIRS * e2, wide), f32),
            pltpu.VMEM((groups, PAIRS * e3, wide), f32),
            pltpu.VMEM((groups, PAIRS * e3, wide), bf16),
            pltpu.VMEM((groups, PAIRS * e3, wide), bf16),
            pltpu.VMEM((groups, PAIRS * e2, wide), f32),
            pltpu.VMEM((groups, PAIRS * e2, wide), bf16),
            pltpu.VMEM((groups, PAIRS * e1, wide), f32),
            pltpu.VMEM((8 * atoms, slots), f32),
            pltpu.VMEM((4 * atoms, slots), f32),
            pltpu.VMEM((8 * atoms, slots), f32),
            pltpu.VMEM((atoms, prepared[10].shape[0]), bf16),
            pltpu.VMEM((4 * prepared[10].shape[0] // e3, atoms, e3), f32),
            pltpu.VMEM((atoms, prepared[10].shape[0]), f32),
            pltpu.VMEM((6, atoms, LANES), f32),
        ],
        compiler_params=pltpu.CompilerParams(vmem_limit_bytes=40 * 1024 * 1024),
        name="evaluate",
    )(rank, before, brick, after, own, *prepared)


def ring(size, step):
    return [(i, (i + step) % size) for i in range(size)]


def flip(size, bit):
    return [(i, i ^ bit) for i in range(size)]


def few(size):
    return size <= 8 and size & (size - 1) == 0


def from_others(value, size):
    return [value] + [lax.ppermute(value, "help", flip(size, k)) for k in range(1, size)]


def gather_help(value):
    size = lax.axis_size("help")
    rank = lax.axis_index("help")
    if not few(size):
        return lax.all_gather(value, "help", axis=1, tiled=True)
    blocks = from_others(value, size)
    bit = 1
    while len(blocks) > 1:
        upper = (rank & bit) != 0
        blocks = [
            jnp.where(
                upper, jnp.concatenate([b, a], axis=1), jnp.concatenate([a, b], axis=1)
            )
            for a, b in zip(blocks[::2], blocks[1::2])
        ]
        bit *= 2
    return blocks[0]


def sum_help(value):
    size = lax.axis_size("help")
    if not few(size):
        return lax.psum(value, "help")
    blocks = from_others(value, size)
    while len(blocks) > 1:
        blocks = [a + b for a, b in zip(blocks[::2], blocks[1::2])]
    return blocks[0]


def exchange(up, down):
    size = lax.axis_size("brick")
    if size % 2:
        return lax.ppermute(up, "brick", ring(size, 1)), lax.ppermute(down, "brick", ring(size, -1))
    odd = (lax.axis_index("brick") & 1) == 1
    inner = lax.ppermute(jnp.where(odd, down, up), "brick", flip(size, 1))
    pairs = [(i, (i + 1) % size if i % 2 else (i - 1) % size) for i in range(size)]
    outer = lax.ppermute(jnp.where(odd, up, down), "brick", pairs)
    return jnp.where(odd, inner, outer), jnp.where(odd, outer, inner)


def local(positions, velocities, forces_in, neighbors, *weights):
    prepared = prepare(neighbors, weights)
    atoms = positions.shape[1]
    rank = lax.axis_index("help")
    ranks = rank.reshape(1).astype(jnp.int32)
    at = rank * atoms
    speed = velocities + kick_scale * forces_in
    coords = positions + time_step * speed
    state = gather_help(jnp.concatenate([coords, speed], axis=0))
    state, made = lax.optimization_barrier((state, prepared[:2]))
    prepared = (*made, *prepared[2:])
    brick_pos, brick_speed = state[:3], state[3:]
    own = coords
    for md_step in range(STEPS):
        before, after = exchange(brick_pos, brick_pos)
        energy, to_before, to_brick, to_after = evaluate(
            ranks, before, brick_pos, after, own, prepared
        )
        from_before, from_after = exchange(to_after, to_before)
        force = sum_help(to_brick + from_before + from_after)
        brick_speed = brick_speed + kick_scale * force
        if md_step + 1 < STEPS:
            brick_speed = brick_speed + kick_scale * force
            brick_pos = brick_pos + time_step * brick_speed
            own = lax.dynamic_slice_in_dim(brick_pos, at, atoms, axis=1)
    out = lax.dynamic_slice_in_dim(
        jnp.concatenate([brick_speed, force], axis=0), at, atoms, axis=1
    )
    return (own, out[:3], energy.reshape(atoms), out[3:])


def solution(mesh):
    spread = ("brick", "help")
    cols = P(None, spread)
    return jax.shard_map(
        local,
        mesh=mesh,
        in_specs=(cols, cols, cols, P(spread, None)) + (P(),) * 11,
        out_specs=(cols, cols, P(spread), cols),
        check_vma=False,
    )
```
